256 devices in a mesh: seq: 8 (over x, core), level: 32 (over y, z).
Axes of the slice: x: 4, y: 4, z: 8, core: 2. Of those that a mesh axis runs over, the one named last changes fastest.
Arguments:
- states: float32 [64, 480, 64, 128], P('seq', 'level'), may hold values from -0.3 to 0.3
- xbc: bfloat16 [64, 8, 1792], P('seq', None, 'level'), may hold values from -1.796875 to 1.796875
- rates: float32 [64, 8, 24], P('seq'), may hold values from 0.02 to 0.8
- level_weights: float32 [64, 8, 480], P('seq', None, 'level'), may hold values from 0.1 to 1
- positions: int32 [64], P('seq'), may hold values from 0 to 1048567, as said below
- accepted: int32 [64], P('seq'), may hold values from 0 to 8
Outputs:
- outputs: bfloat16 [64, 8, 1536], P('seq', None, 'level')
- new_states: float32 [64, 480, 64, 128], P('seq', 'level')
- acceptance: float32 [], replicated
The draws below stay inside these ranges and needn't reach their ends.
Inputs may be any that keep to these rules, and one draw needn't show every extreme that they name: `positions`: p + 8 stays below 2**20.
All inputs are finite; a program needn't handle non-finite values.
Results may differ from the reference program's by a relative error of at most 0.0019.
Values may be sent and summed in bfloat16 or wider, within the bound.
A program may use at most 64 MiB of HBM per device.

```python
import math
import jax
import jax.numpy as jnp
from jax import lax

H = 24
P_SIZE = 64
N = 128
L = 20
K = 8
SEQS = 64


def draw_positions(key, part):
    lowest_bit = (K - 1).bit_length()
    keys = jax.random.split(jax.random.fold_in(key, 7), 3)
    bit_power = jax.random.randint(keys[0], (SEQS,), lowest_bit, L, dtype=jnp.int32)
    step_back = jax.random.randint(keys[1], (SEQS,), 1, K + 1, dtype=jnp.int32)
    ceiling = jnp.left_shift(jnp.int32(1), L - bit_power)
    multiple = jax.random.randint(keys[2], (SEQS,), 1, ceiling, dtype=jnp.int32)
    return (multiple * jnp.left_shift(jnp.int32(1), bit_power) - step_back).astype(jnp.int32)


def place_ends(values, rng, smallest, high):
    shape = values.shape
    spot = [jax.random.randint(jax.random.fold_in(rng, axis), (), 0, shape[axis]) for axis in range(len(shape))]
    values = values.at[tuple(spot)].set(smallest)
    longest = shape.index(max(shape))
    spot[longest] = (spot[longest] + 1) % shape[longest]
    return values.at[tuple(spot)].set(high)


def shard_levels(key, shape, shards, least, high):
    def one(dim, shards_of):
        steps = jax.random.uniform(jax.random.fold_in(jax.random.fold_in(key, 6), dim), (shards_of,), jnp.float32, least / len(shards), high / len(shards))
        return jnp.repeat(jnp.exp(steps), shape[dim] // shards_of).reshape((-1,) + (1,) * (len(shape) - dim - 1))

    level = one(*shards[0])
    for cut in shards[1:]:
        level = level * one(*cut)
    return level


def gaussian(own_key, dims, scale, bound, shards=(), held_as=jnp.bfloat16):
    array = scale * jax.random.normal(own_key, dims, jnp.float32)
    if shards:
        array = array * shard_levels(own_key, dims, shards, -0.22, 0.18)
    return jnp.clip(array, -bound, bound).astype(held_as)


def setup_inputs(seed: int = 0) -> dict:
    arg_keys = jax.random.split(jax.random.key(seed), 7)
    states = gaussian(arg_keys[0], (SEQS, H * L, P_SIZE, N), 0.05, 0.3, ((0, 8), (1, 32)), jnp.float32)
    xbc = gaussian(arg_keys[1], (SEQS, K, H * P_SIZE + 2 * N), 0.3, 1.796875, ((0, 8), (2, 32)))
    rates = jnp.clip(jnp.exp(math.log(0.8) - 3.6888795 * jax.random.uniform(arg_keys[2], (SEQS, K, H), jnp.float32) ** shard_levels(arg_keys[2], (SEQS, K, H), ((0, 8),), -0.2, 0.2)), 0.02, 0.8)
    level_weights = jnp.clip(jnp.exp(math.log(1.0) - 2.3025851 * jax.random.uniform(arg_keys[3], (SEQS, K, H * L), jnp.float32) ** shard_levels(arg_keys[3], (SEQS, K, H * L), ((0, 8), (2, 32)), -0.2, 0.2)), 0.1, 1.0)
    positions = draw_positions(jax.random.fold_in(arg_keys[6], 71), 0)
    accepted = place_ends(jax.random.randint(arg_keys[5], (SEQS,), 0, K + 1), jax.random.fold_in(arg_keys[5], 1), 0, K).astype(jnp.int32)
    return dict(states=states, xbc=xbc, rates=rates, level_weights=level_weights, positions=positions, accepted=accepted)


def one_sequence(inputs_one):
    highest = lax.Precision.HIGHEST
    offset = L // 2
    block, drafts, decay_rates, weights_one, position, taken = inputs_one
    values = drafts[:, :H * P_SIZE].astype(jnp.float32).reshape(K, H, P_SIZE)
    in_vecs = drafts[:, H * P_SIZE:H * P_SIZE + N].astype(jnp.float32)
    out_vecs = drafts[:, H * P_SIZE + N:].astype(jnp.float32)
    cumul = jnp.cumsum(-decay_rates, axis=0)
    levels = jnp.arange(L, dtype=jnp.int32)
    occupied = (jnp.right_shift(position, levels) % 2).astype(jnp.float32)
    level_states = jnp.roll(block, offset, axis=0).reshape(H, L, P_SIZE, N)
    weights = jnp.roll(weights_one, offset, axis=1).reshape(K, H, L)
    readout = jnp.einsum('hlpn,tn->thlp', level_states, out_vecs, precision=highest)
    factor = weights * occupied[None, None, :] * jnp.exp(cumul)[:, :, None]
    from_states = jnp.sum(factor[..., None] * readout, axis=2)
    steps_all = jnp.arange(K, dtype=jnp.int32)
    causal = steps_all[None, :] <= steps_all[:, None]
    scores = jnp.dot(out_vecs, in_vecs.T, precision=highest)
    spread = cumul[:, None, :] - cumul[None, :, :]
    mixing = jnp.where(causal[:, :, None], jnp.exp(jnp.minimum(spread, 0.0)), 0.0) * scores[:, :, None]
    from_drafts = weights[:, :, 0][..., None] * jnp.einsum('tuh,uhp->thp', mixing, values, precision=highest)
    result = (from_states + from_drafts).reshape(K, H * P_SIZE).astype(jnp.bfloat16)
    new_position = position + taken
    new_occupied = (jnp.right_shift(new_position, levels) % 2).astype(jnp.float32)
    changed = jnp.bitwise_xor(position, new_position)
    top_level = jnp.sum((jnp.right_shift(changed, levels) > 0).astype(jnp.int32)) - 1
    staying = occupied * (levels > top_level).astype(jnp.float32)
    leaving = occupied * (levels < top_level).astype(jnp.float32)
    moved = jnp.sum(leaving[None, :, None, None] * level_states, axis=1)
    target = (levels == top_level).astype(jnp.float32)
    merged = staying[None, :, None, None] * level_states + target[None, :, None, None] * moved[:, None]
    live = (steps_all < taken).astype(jnp.float32)
    cum_taken = jnp.sum(-decay_rates * live[:, None], axis=0)
    token_pos = position + steps_all
    start_new = jnp.left_shift(jnp.right_shift(new_position, levels + 1), levels + 1)
    level_span = jnp.left_shift(jnp.int32(1), levels)
    inside = ((token_pos[None, :] >= start_new[:, None]) & (token_pos[None, :] < start_new[:, None] + level_span[:, None])).astype(jnp.float32) * live[None, :]
    token_decay = jnp.exp(jnp.minimum(cum_taken[None, :] - cumul, 0.0)) * live[:, None]
    tokens = jnp.einsum('lu,uh,uhp,un->hlpn', inside, token_decay, values, in_vecs, precision=highest)
    updated = new_occupied[None, :, None, None] * (jnp.exp(cum_taken)[:, None, None, None] * merged + tokens)
    return result, jnp.roll(updated.reshape(H * L, P_SIZE, N), -offset, axis=0)


def reference(states, xbc, rates, level_weights, positions, accepted):
    outputs, new_states = lax.map(one_sequence, (states, xbc, rates, level_weights, positions, accepted))
    acceptance = jnp.sum(accepted.astype(jnp.float32)) / (SEQS * K)
    return outputs, new_states, acceptance
```

```python
import functools

import jax
import jax.numpy as jnp
from jax import lax
from jax.experimental import pallas as pl
from jax.experimental.pallas import tpu as pltpu
from jax.sharding import PartitionSpec as P

H = 24
P_SIZE = 64
N = 128
L = 20
K = 8
ROW = 8
OWN_IN = 56
OWN_OUT = 48
LOCAL = 15
BC_FIRST = 27
BC_SLOTS = 5
X_LOW, X_HIGH = -5, 2
MESH = pl.DeviceIdType.MESH
F32 = jnp.float32
BF16 = jnp.bfloat16


def first_head_of(d):
    return lax.rem(lax.div(LOCAL * d + L // 2, L), H)


def first_level_of(d):
    return lax.rem(LOCAL * d + L // 2, L)


def heads_of(d):
    return jnp.where(first_level_of(d) + LOCAL > L, 2, 1)


def value_offset(d, s):
    u = OWN_IN * s - P_SIZE * first_head_of(d)
    return jnp.where(u < -(H * P_SIZE) // 2, u + H * P_SIZE, u)


def needs_values(d, s):
    u = value_offset(d, s)
    return (s <= BC_FIRST) & (u > -OWN_IN) & (u < P_SIZE * heads_of(d))


def wrapped(d, devices):
    return lax.rem(d + devices, devices)


def as_int(x):
    return x.astype(jnp.int32)


def split_two(x):
    high = x.astype(BF16).astype(F32)
    return high, x - high


def kernel(
    devices,
    groups,
    states_ref,
    xbc_ref,
    rates_ref,
    weights_ref,
    pos_ref,
    acc_ref,
    out_ref,
    new_ref,
    share_ref,
    held,
    halves,
    made,
    padded,
    piece,
    bc,
    xs,
    low_send,
    low_recv,
    low_a,
    low_b,
    leave_c,
    stay_c,
    into_c,
    wide_w,
    cc,
    bb,
    xg,
    psend,
    pslots,
    counts,
    in_sem,
    new_sem,
    y_send,
    z_send,
    x_send,
    bc_recv,
    x_recv,
    low_sems,
    p_send,
    p_recv,
    n_send,
    n_recv,
):
    seqs = xbc_ref.shape[0]
    rows = seqs * K
    me = lax.axis_index("level")
    sq = lax.axis_index("seq")
    y, z = lax.div(me, ROW), lax.rem(me, ROW)
    columns = devices // ROW
    first_z = BC_FIRST - (columns - 1) * ROW
    has_slot = z >= first_z
    is_source = has_slot & (y == columns - 1)
    kind = lax.rem(me, 4)
    slot = jnp.maximum(z - first_z, 0)

    barrier = pltpu.get_barrier_semaphore()

    def greet(group, level):
        pl.semaphore_signal(barrier, inc=1, device_id=(group, level), device_id_type=MESH)

    for other in range(first_z, ROW):

        @pl.when(z != other)
        def _():
            greet(sq, y * ROW + other)

    @pl.when(has_slot & (y != columns - 1))
    def _():
        greet(sq, (columns - 1) * ROW + z)

    for gap in range(X_LOW, X_HIGH + 1):
        if gap != 0:
            source = wrapped(me + gap, devices)

            @pl.when(needs_values(me, source))
            def _():
                greet(sq, source)

    greet(sq, wrapped(me - 1, devices))

    @pl.when((kind == 1) | (kind == 2))
    def _():
        greet(sq, wrapped(me - 2, devices))

    @pl.when(kind == 2)
    def _():
        greet(sq, wrapped(me + 1, devices))

    for step in range(1, groups):
        greet(lax.rem(sq + step, groups), me)

    expected = 7 * as_int(has_slot) + (columns - 1) * as_int(is_source) + groups
    for gap in range(X_LOW, X_HIGH + 1):
        if gap != 0:
            expected = expected + as_int(needs_values(wrapped(me - gap, devices), me))
    expected = expected + as_int((kind == 0) | (kind == 3)) + as_int(kind == 3)

    def load(s):
        return pltpu.make_async_copy(states_ref.at[s], held.at[s], in_sem.at[s])

    for s in range(seqs):
        load(s).start()

    lane = lax.broadcasted_iota(jnp.int32, (rows, 128), 1)
    lower = lane < P_SIZE
    half_rows = rows // 2
    half_lane = lane[:half_rows]
    half_lower = half_lane < P_SIZE

    padded[...] = jnp.zeros_like(padded)
    padded[:, 0:OWN_IN] = xbc_ref[...].astype(F32).reshape(rows, OWN_IN)
    wide = padded[...]
    packed = jnp.where(half_lower, wide[:half_rows], pltpu.roll(wide[half_rows:], P_SIZE, 1))
    packed = packed.astype(BF16)
    piece[...] = packed
    xs[-X_LOW] = packed

    @pl.when(is_source)
    def _():
        bc[slot] = packed

    sub = lax.broadcasted_iota(jnp.int32, (seqs, 128), 0)
    pos_s = jnp.zeros((seqs, 128), jnp.int32)
    acc_s = jnp.zeros((seqs, 128), jnp.int32)
    for s in range(seqs):
        pos_s = jnp.where(sub == s, pos_ref[s], pos_s)
        acc_s = jnp.where(sub == s, acc_ref[s], acc_s)
    new_s = pos_s + acc_s
    changed = pos_s ^ new_s
    level_0 = first_level_of(me)
    split = jnp.minimum(L - level_0, LOCAL)
    levels = [lax.rem(level_0 + j, L) for j in range(LOCAL)] + [0]
    for j in range(LOCAL):
        occupied = (pos_s >> levels[j]) & 1
        above = changed >> levels[j]
        leave_c[j] = jnp.where((above >> 1) != 0, occupied, 0).astype(F32)

    block = LOCAL // 3
    halves[:, LOCAL * P_SIZE :, :] = jnp.zeros((seqs, P_SIZE, 2 * N), BF16)
    has_zero_in_a = level_0 == 0

    def gather_low(s, carry):
        load(s).wait()
        sums = []
        for part in range(3):
            total = None
            for j in range(part * block, (part + 1) * block):
                x = held[s, j * P_SIZE : (j + 1) * P_SIZE, :]
                high, low = split_two(x)
                halves[s, j * P_SIZE : (j + 1) * P_SIZE, 0:N] = high.astype(BF16)
                halves[s, j * P_SIZE : (j + 1) * P_SIZE, N : 2 * N] = low.astype(BF16)
                term = x * leave_c[j, pl.ds(s, 1), :]
                total = term if total is None else total + term
            sums.append(total)
        zero = jnp.zeros_like(sums[0])
        one_in_a, two_in_a = split > block, split > 2 * block
        in_a = sums[0] + jnp.where(one_in_a, sums[1], zero) + jnp.where(two_in_a, sums[2], zero)
        in_b = jnp.where(one_in_a, zero, sums[1]) + jnp.where(two_in_a, zero, sums[2])
        low_a[s] = in_a
        low_b[s] = in_b
        low_send[s] = jnp.where(has_zero_in_a, in_a, in_b).astype(BF16)
        return carry

    lax.fori_loop(0, seqs, gather_low, 0)

    taken_here = jnp.int32(0)
    for s in range(seqs):
        taken_here = taken_here + acc_ref[s]
    counts[sq] = jnp.full((8, 128), taken_here, jnp.int32).astype(F32)

    pl.semaphore_wait(barrier, expected)

    def remote(src, dst, send_sem, recv_sem, group, level):
        return pltpu.make_async_remote_copy(
            src_ref=src,
            dst_ref=dst,
            send_sem=send_sem,
            recv_sem=recv_sem,
            device_id=(group, level),
            device_id_type=MESH,
        )

    def y_copy(row):
        return remote(bc.at[slot], bc.at[slot], y_send.at[row], bc_recv.at[slot], sq, row * ROW + z)

    def z_copy(step):
        other = y * ROW + lax.rem(z + step, ROW)
        return remote(bc.at[slot], bc.at[slot], z_send.at[step], bc_recv.at[slot], sq, other)

    def x_copy(gap):
        target = wrapped(me - gap, devices)
        index = gap - X_LOW
        return remote(piece, xs.at[index], x_send.at[index], x_recv.at[index], sq, target)

    def low_copy():
        target = wrapped(me + 1, devices)
        return remote(low_send, low_recv, low_sems.at[0], low_sems.at[1], sq, target)

    def count_copy(step):
        return remote(
            counts.at[sq], counts.at[sq], n_send.at[step], n_recv.at[sq], lax.rem(sq + step, groups), me
        )

    def partial_copy(index, gap):
        target = wrapped(me + gap, devices)
        return remote(psend, pslots.at[index], p_send.at[index], p_recv.at[index], sq, target)

    sends_low = kind != 1
    gets_low = kind != 2
    gaps = [gap for gap in range(X_LOW, X_HIGH + 1) if gap != 0]
    near = (
        (0, 1, None, None),
        (1, 2, (kind == 0) | (kind == 3), (kind == 1) | (kind == 2)),
        (2, -1, kind == 3, kind == 2),
    )

    def when(cond, do):
        if cond is None:
            do()
        else:
            pl.when(cond)(do)

    @pl.when(is_source)
    def _():
        for row in range(columns - 1):
            y_copy(row).start()

    for gap in gaps:
        when(needs_values(wrapped(me - gap, devices), me), lambda: x_copy(gap).start())
    when(sends_low, lambda: low_copy().start())
    for step in range(1, groups):
        count_copy(step).start()

    head_lane = lax.broadcasted_iota(jnp.int32, (rows, H), 1)
    rates = rates_ref[...].reshape(rows, H)
    first_head = first_head_of(me)
    second_head = lax.rem(first_head + 1, H)
    row = lax.broadcasted_iota(jnp.int32, (rows, 128), 0)
    token = row & (K - 1)
    pos_rows = jnp.concatenate([jnp.full((K, 128), pos_ref[s], jnp.int32) for s in range(seqs)], 0)
    acc_rows = jnp.concatenate([jnp.full((K, 128), acc_ref[s], jnp.int32) for s in range(seqs)], 0)
    new_rows = pos_rows + acc_rows
    token_rows = pos_rows + token
    live = token < acc_rows

    def decays(head):
        rate = jnp.sum(jnp.where(head_lane == head, rates, 0.0), axis=1, keepdims=True)
        rate = jnp.broadcast_to(rate, (rows, 128))
        running = rate
        for by in (1, 2, 4):
            running = running + jnp.where(token >= by, pltpu.roll(running, by, 0), 0.0)
        cum = -running
        taken = -jnp.sum(jnp.where(live, rate, 0.0).reshape(seqs, K, 128), axis=1)
        taken_rows = jnp.broadcast_to(taken[:, None, :], (seqs, K, 128)).reshape(rows, 128)
        decay = jnp.where(live, jnp.exp(jnp.minimum(taken_rows - cum, 0.0)), 0.0)
        return cum, jnp.exp(cum), jnp.exp(taken), decay

    cum_a, grown_a, kept_a, decay_a = decays(first_head)
    cum_b, grown_b, kept_b, decay_b = decays(second_head)

    for j in range(LOCAL):
        in_a = j < split
        kept = jnp.where(in_a, kept_a, kept_b)
        occupied = (pos_s >> levels[j]) & 1
        new_occupied = (new_s >> levels[j]) & 1
        above = changed >> levels[j]
        stay_c[j] = jnp.where((above == 0) & (occupied == 1) & (new_occupied == 1), kept, 0.0)
        into_c[j] = jnp.where((above == 1) & (new_occupied == 1), kept, 0.0)

    weights = weights_ref[...].reshape(rows, LOCAL)
    local_lane = lax.broadcasted_iota(jnp.int32, (rows, LOCAL), 1)
    level_lane = lax.rem(level_0 + local_lane, L)
    weight_zero = jnp.sum(jnp.where(level_lane == 0, weights, 0.0), axis=1, keepdims=True)
    quads = (LOCAL + 1) // 2

    def of_lane(q):
        two = 2 * q + jnp.where(lower, 0, 1)
        return jnp.where(lower, levels[2 * q], levels[2 * q + 1]), two < split, two < LOCAL

    for q in range(quads):
        level, in_a, real = of_lane(q)
        first = jnp.broadcast_to(weights[:, 2 * q : 2 * q + 1], (rows, 128))
        if 2 * q + 1 < LOCAL:
            second = jnp.broadcast_to(weights[:, 2 * q + 1 : 2 * q + 2], (rows, 128))
        else:
            second = jnp.zeros((rows, 128), F32)
        occupied = ((pos_rows >> level) & 1) == 1
        grown = jnp.where(in_a, grown_a, grown_b)
        wide_w[q] = jnp.where(occupied & real, jnp.where(lower, first, second) * grown, 0.0)

    @pl.when(has_slot)
    def _():
        @pl.when(y != columns - 1)
        def _():
            remote(
                bc.at[slot], bc.at[slot], y_send.at[0], bc_recv.at[slot], sq, me
            ).wait_recv()

        for step in range(1, ROW):
            z_copy(step).start()

    for other in range(first_z, ROW):
        index = other - first_z

        @pl.when(z != other)
        def _():
            remote(
                bc.at[index], bc.at[index], y_send.at[0], bc_recv.at[index], sq, me
            ).wait_recv()

    got = [bc[i].astype(F32) for i in range(BC_SLOTS)]

    def vectors(first_feature):
        parts = []
        for r in range(2):
            part = jnp.zeros((half_rows, 128), F32)
            for i in range(BC_SLOTS):
                start = OWN_IN * (BC_FIRST + i) - first_feature
                if start > -OWN_IN and start < N:
                    moved = got[i]
                    by = (start - P_SIZE * r) % 128
                    if by:
                        moved = pltpu.roll(moved, by, 1)
                    part = jnp.where((half_lane >= start) & (half_lane < start + OWN_IN), moved, part)
            parts.append(part)
        return jnp.concatenate(parts, axis=0)

    in_vecs = vectors(H * P_SIZE)
    out_vecs = vectors(H * P_SIZE + N)
    c3 = out_vecs.reshape(seqs, K, N)
    c3 = jnp.concatenate([c3, jnp.zeros_like(c3)], axis=1).astype(BF16)
    cc[:, :, 0:N] = c3
    cc[:, :, N : 2 * N] = c3

    for gap in gaps:
        index = gap - X_LOW
        source = wrapped(me + gap, devices)
        when(
            needs_values(me, source),
            lambda: remote(
                piece, xs.at[index], x_send.at[index], x_recv.at[index], sq, me
            ).wait_recv(),
        )
    value_parts = []
    for r in range(2):
        part = jnp.zeros((half_rows, 128), F32)
        for gap in range(X_LOW, X_HIGH + 1):
            source = wrapped(me + gap, devices)
            start = value_offset(me, source)
            end = start + jnp.minimum(OWN_IN, H * P_SIZE - OWN_IN * source)
            wanted = needs_values(me, source)
            first = jnp.where(wanted, start, 128)
            by = lax.rem(start + 4 * H * P_SIZE - P_SIZE * r, 128)
            moved = pltpu.roll(xs[gap - X_LOW].astype(F32), by, 1)
            part = jnp.where((half_lane >= first) & (half_lane < end), moved, part)
        value_parts.append(part)
    values = jnp.concatenate(value_parts, axis=0)

    b16 = in_vecs.astype(BF16)
    scores = lax.dot_general(
        out_vecs.astype(BF16),
        jnp.concatenate([b16, b16], axis=0),
        (((1,), (1,)), ((), ())),
        preferred_element_type=F32,
    )
    cum_zero = jnp.where(has_zero_in_a, cum_a, cum_b)
    source_row = lane & (rows - 1)
    cum_across = jnp.sum(jnp.where(source_row == row, cum_zero, 0.0), axis=0, keepdims=True)
    before = ((source_row >> 3) == (row >> 3)) & (source_row <= row)
    mixing = jnp.where(before, jnp.exp(jnp.minimum(cum_zero - cum_across, 0.0)), 0.0) * scores
    high, low = split_two(mixing)
    v16 = values.astype(BF16)
    mixed = jnp.dot(
        jnp.where(lower, high, low).astype(BF16),
        jnp.concatenate([v16, v16], axis=0),
        preferred_element_type=F32,
    )
    zero_here = jnp.where(lower, 1, 0) == as_int(has_zero_in_a)
    psend[...] = jnp.where(zero_here, mixed * weight_zero, 0.0)

    lane8 = lane[:K]
    lower8 = lane8 < P_SIZE

    def read_out(s, carry):
        read = lax.dot_general(
            cc[s], halves[s], (((1,), (1,)), ((), ())), preferred_element_type=F32
        )
        sum_a = jnp.zeros((K, 128), F32)
        sum_b = jnp.zeros((K, 128), F32)
        at = pl.ds(pl.multiple_of(s * K, K), K)
        for q in range(quads):
            two = 2 * q + jnp.where(lower8, 0, 1)
            term = read[:K, q * 128 : (q + 1) * 128] * wide_w[q, at, :]
            sum_a = sum_a + jnp.where(two < split, term, 0.0)
            sum_b = sum_b + jnp.where(two < split, 0.0, term)
        sum_a = sum_a + pltpu.roll(sum_a, P_SIZE, 1)
        sum_b = sum_b + pltpu.roll(sum_b, P_SIZE, 1)
        psend[at, :] = psend[at, :] + jnp.where(lower8, sum_a, sum_b)
        return carry

    lax.fori_loop(0, seqs, read_out, 0)

    for index, gap, sends, _ in near:
        when(sends, lambda: partial_copy(index, gap).start())

    turned = pltpu.roll(values, P_SIZE, 1)
    values_a = jnp.where(lower, values, turned) * decay_a
    values_b = jnp.where(lower, turned, values) * decay_b
    b3 = in_vecs.reshape(seqs, K, N)
    bb[...] = jnp.concatenate([b3, b3], axis=1).astype(BF16)
    for q in range(quads):
        level, in_a, real = of_lane(q)
        until = new_rows >> level
        inside = ((until & 1) == 1) & ((token_rows >> level) + 1 == until) & live & real
        term = jnp.where(inside, jnp.where(in_a, values_a, values_b), 0.0)
        high, low = split_two(term)
        both = jnp.concatenate(
            [high.reshape(seqs, K, 128), low.reshape(seqs, K, 128)], axis=1
        )
        xg[:, :, q * 128 : (q + 1) * 128] = both.astype(BF16)

    when(gets_low, lambda: low_copy().wait_recv())

    def store(s):
        return pltpu.make_async_copy(made.at[s], new_ref.at[s], new_sem.at[s])

    def update(s, carry):
        tokens = lax.dot_general(
            xg[s], bb[s], (((0,), (0,)), ((), ())), preferred_element_type=F32
        )
        came = jnp.where(gets_low, low_recv[s].astype(F32), 0.0)
        merged_a = low_a[s] + came
        merged_b = low_b[s]
        merged = (
            merged_a,
            jnp.where(split > block, merged_a, merged_b),
            jnp.where(split > 2 * block, merged_a, merged_b),
        )
        for j in range(LOCAL):
            at = slice(j * P_SIZE, (j + 1) * P_SIZE)
            made[s, at, :] = (
                held[s, at, :] * stay_c[j, pl.ds(s, 1), :]
                + merged[j // block] * into_c[j, pl.ds(s, 1), :]
                + tokens[at, :]
            )
        store(s).start()
        return carry

    lax.fori_loop(0, seqs, update, 0)

    for index, gap, _, gets in near:
        when(
            gets,
            lambda: remote(
                psend, pslots.at[index], p_send.at[index], p_recv.at[index], sq, me
            ).wait_recv(),
        )
    total = jnp.zeros((rows, 128), F32)
    sources = [(None, 0, None)] + [(index, -gap, gets) for index, gap, _, gets in near]
    for index, gap, gets in sources:
        source = wrapped(me + gap, devices)
        offset = OWN_OUT * me - P_SIZE * first_head_of(source)
        offset = jnp.where(offset < -(H * P_SIZE) // 2, offset + H * P_SIZE, offset)
        offset = jnp.where(offset > (H * P_SIZE) // 2, offset - H * P_SIZE, offset)
        by = lax.rem(4 * H * P_SIZE - offset, 128)
        end = P_SIZE * heads_of(source)
        if gets is not None:
            end = jnp.where(gets, end, -(1 << 20))
        moved = pltpu.roll(psend[...] if index is None else pslots[index], by, 1)
        total = total + jnp.where((lane + offset >= 0) & (lane + offset < end), moved, 0.0)
    out_ref[...] = total.reshape(seqs, K, 128)[:, :, 0:OWN_OUT].astype(BF16)

    for step in range(1, groups):
        other = lax.rem(sq + step, groups)
        remote(
            counts.at[other], counts.at[other], n_send.at[step], n_recv.at[other], sq, me
        ).wait_recv()
    taken = jnp.sum(counts[...], axis=0)
    share_ref[...] = taken[0:1, 0:1] / (groups * seqs * K)

    @pl.when(is_source)
    def _():
        for r in range(columns - 1):
            y_copy(r).wait_send()

    @pl.when(has_slot)
    def _():
        for step in range(1, ROW):
            z_copy(step).wait_send()

    for gap in gaps:
        when(needs_values(wrapped(me - gap, devices), me), lambda: x_copy(gap).wait_send())
    when(sends_low, lambda: low_copy().wait_send())
    for step in range(1, groups):
        count_copy(step).wait_send()
    for index, gap, sends, _ in near:
        when(sends, lambda: partial_copy(index, gap).wait_send())
    for s in range(seqs):
        store(s).wait()


def on_device(states, xbc, rates, level_weights, positions, accepted):
    devices = lax.axis_size("level")
    groups = lax.axis_size("seq")
    seqs = states.shape[0]
    rows = seqs * K
    wide = LOCAL * P_SIZE
    padded_wide = (LOCAL + 1) * P_SIZE
    vmem = pl.BlockSpec(memory_space=pltpu.VMEM)
    smem = pl.BlockSpec(memory_space=pltpu.SMEM)
    anywhere = pl.BlockSpec(memory_space=pl.ANY)
    in_hbm = pl.BlockSpec(memory_space=pltpu.HBM)
    dma = pltpu.SemaphoreType.DMA
    x_slots = X_HIGH - X_LOW + 1
    outputs, new_states, share = pl.pallas_call(
        functools.partial(kernel, devices, groups),
        out_shape=(
            jax.ShapeDtypeStruct((seqs, K, OWN_OUT), BF16),
            jax.ShapeDtypeStruct((seqs, wide, N), F32),
            jax.ShapeDtypeStruct((1, 1), F32),
        ),
        in_specs=[in_hbm, vmem, vmem, vmem, smem, smem],
        out_specs=(vmem, anywhere, vmem),
        scratch_shapes=[
            pltpu.VMEM((seqs, wide, N), F32),
            pltpu.VMEM((seqs, padded_wide, 2 * N), BF16),
            pltpu.VMEM((seqs, wide, N), F32),
            pltpu.VMEM((rows, 128), F32),
            pltpu.VMEM((rows // 2, 128), BF16),
            pltpu.VMEM((BC_SLOTS, rows // 2, 128), BF16),
            pltpu.VMEM((x_slots, rows // 2, 128), BF16),
            pltpu.VMEM((seqs, P_SIZE, N), BF16),
            pltpu.VMEM((seqs, P_SIZE, N), BF16),
            pltpu.VMEM((seqs, P_SIZE, N), F32),
            pltpu.VMEM((seqs, P_SIZE, N), F32),
            pltpu.VMEM((LOCAL, seqs, 128), F32),
            pltpu.VMEM((LOCAL, seqs, 128), F32),
            pltpu.VMEM((LOCAL, seqs, 128), F32),
            pltpu.VMEM(((LOCAL + 1) // 2, rows, 128), F32),
            pltpu.VMEM((seqs, 2 * K, 2 * N), BF16),
            pltpu.VMEM((seqs, 2 * K, N), BF16),
            pltpu.VMEM((seqs, 2 * K, padded_wide), BF16),
            pltpu.VMEM((rows, 128), F32),
            pltpu.VMEM((3, rows, 128), F32),
            pltpu.VMEM((groups, 8, 128), F32),
            dma((seqs,)),
            dma((seqs,)),
            dma((devices // ROW,)),
            dma((ROW,)),
            dma((x_slots,)),
            dma((BC_SLOTS,)),
            dma((x_slots,)),
            dma((2,)),
            dma((3,)),
            dma((3,)),
            dma((groups,)),
            dma((groups,)),
        ],
        compiler_params=pltpu.CompilerParams(
            collective_id=0, has_side_effects=True, vmem_limit_bytes=40 << 20
        ),
    )(
        states.reshape(seqs, wide, N),
        xbc,
        rates,
        level_weights,
        positions,
        accepted,
    )
    return outputs, new_states.reshape(states.shape), share.reshape(())


def solution(mesh):
    in_specs = (
        P("seq", "level", None, None),
        P("seq", None, "level"),
        P("seq", None, None),
        P("seq", None, "level"),
        P("seq"),
        P("seq"),
    )
    out_specs = (P("seq", None, "level"), P("seq", "level", None, None), P())
    return jax.shard_map(
        on_device, mesh=mesh, in_specs=in_specs, out_specs=out_specs, check_vma=False
    )
```

```python
import functools

import jax
import jax.numpy as jnp
from jax import lax
from jax.experimental import pallas as pl
from jax.experimental.pallas import tpu as pltpu
from jax.sharding import PartitionSpec as P

H = 24
P_SIZE = 64
N = 128
L = 20
K = 8
ROW = 8
OWN_IN = 56
OWN_OUT = 48
LOCAL = 15
BC_FIRST = 27
BC_SLOTS = 5
X_LOW, X_HIGH = -5, 2
MESH = pl.DeviceIdType.MESH
F32 = jnp.float32
BF16 = jnp.bfloat16


def first_head_of(d):
    return lax.rem(lax.div(LOCAL * d + L // 2, L), H)


def first_level_of(d):
    return lax.rem(LOCAL * d + L // 2, L)


def heads_of(d):
    return jnp.where(first_level_of(d) + LOCAL > L, 2, 1)


def value_offset(d, s):
    u = OWN_IN * s - P_SIZE * first_head_of(d)
    return jnp.where(u < -(H * P_SIZE) // 2, u + H * P_SIZE, u)


def needs_values(d, s):
    u = value_offset(d, s)
    return (s <= BC_FIRST) & (u > -OWN_IN) & (u < P_SIZE * heads_of(d))


def wrapped(d, devices):
    return lax.rem(d + devices, devices)


def as_int(x):
    return x.astype(jnp.int32)


def split_two(x):
    high = x.astype(BF16).astype(F32)
    return high, x - high


def kernel(
    devices,
    groups,
    states_ref,
    xbc_in,
    rates_in,
    weights_in,
    pos_in,
    acc_in,
    out_ref,
    new_ref,
    share_ref,
    xbc_ref,
    rates_ref,
    weights_ref,
    pos_ref,
    acc_ref,
    held,
    halves,
    padded,
    piece,
    bc,
    xs,
    low_send,
    low_recv,
    low_a,
    low_b,
    leave_c,
    stay_c,
    into_c,
    wide_w,
    cc,
    bb,
    xg,
    psend,
    pslots,
    counts,
    small_sem,
    in_sem,
    y_send,
    z_send,
    x_send,
    bc_recv,
    x_recv,
    low_sems,
    p_send,
    p_recv,
    n_send,
    n_recv,
):
    seqs = xbc_ref.shape[0]
    rows = seqs * K
    me = lax.axis_index("level")
    sq = lax.axis_index("seq")
    y, z = lax.div(me, ROW), lax.rem(me, ROW)
    columns = devices // ROW
    first_z = BC_FIRST - (columns - 1) * ROW
    has_slot = z >= first_z
    is_source = has_slot & (y == columns - 1)
    kind = lax.rem(me, 4)
    slot = jnp.maximum(z - first_z, 0)

    small = [
        pltpu.make_async_copy(src, dst, small_sem.at[i])
        for i, (src, dst) in enumerate(
            (
                (xbc_in, xbc_ref),
                (pos_in, pos_ref),
                (acc_in, acc_ref),
                (rates_in, rates_ref),
                (weights_in, weights_ref),
            )
        )
    ]

    def load(s):
        return pltpu.make_async_copy(states_ref.at[s], held.at[s], in_sem.at[s])

    for copy in small:
        copy.start()
    for s in range(seqs):
        load(s).start()

    barrier = pltpu.get_barrier_semaphore()

    def greet(group, level):
        pl.semaphore_signal(barrier, inc=1, device_id=(group, level), device_id_type=MESH)

    for other in range(first_z, ROW):

        @pl.when(z != other)
        def _():
            greet(sq, y * ROW + other)

    @pl.when(has_slot & (y != columns - 1))
    def _():
        greet(sq, (columns - 1) * ROW + z)

    for gap in range(X_LOW, X_HIGH + 1):
        if gap != 0:
            source = wrapped(me + gap, devices)

            @pl.when(needs_values(me, source))
            def _():
                greet(sq, source)

    greet(sq, wrapped(me - 1, devices))

    @pl.when((kind == 1) | (kind == 2))
    def _():
        greet(sq, wrapped(me - 2, devices))

    @pl.when(kind == 2)
    def _():
        greet(sq, wrapped(me + 1, devices))

    for step in range(1, groups):
        greet(lax.rem(sq + step, groups), me)

    expected = 7 * as_int(has_slot) + (columns - 1) * as_int(is_source) + groups
    for gap in range(X_LOW, X_HIGH + 1):
        if gap != 0:
            expected = expected + as_int(needs_values(wrapped(me - gap, devices), me))
    expected = expected + as_int((kind == 0) | (kind == 3)) + as_int(kind == 3)

    lane = lax.broadcasted_iota(jnp.int32, (rows, 128), 1)
    lower = lane < P_SIZE
    half_rows = rows // 2
    half_lane = lane[:half_rows]
    half_lower = half_lane < P_SIZE

    padded[...] = jnp.zeros_like(padded)
    small[0].wait()
    padded[:, 0:OWN_IN] = xbc_ref[...].astype(F32).reshape(rows, OWN_IN)
    wide = padded[...]
    packed = jnp.where(half_lower, wide[:half_rows], pltpu.roll(wide[half_rows:], P_SIZE, 1))
    packed = packed.astype(BF16)
    piece[...] = packed
    xs[-X_LOW] = packed

    @pl.when(is_source)
    def _():
        bc[slot] = packed

    small[1].wait()
    small[2].wait()
    sub = lax.broadcasted_iota(jnp.int32, (seqs, 128), 0)
    pos_s = jnp.zeros((seqs, 128), jnp.int32)
    acc_s = jnp.zeros((seqs, 128), jnp.int32)
    for s in range(seqs):
        pos_s = jnp.where(sub == s, pos_ref[s], pos_s)
        acc_s = jnp.where(sub == s, acc_ref[s], acc_s)
    new_s = pos_s + acc_s
    changed = pos_s ^ new_s
    level_0 = first_level_of(me)
    split = jnp.minimum(L - level_0, LOCAL)
    levels = [lax.rem(level_0 + j, L) for j in range(LOCAL)] + [0]
    for j in range(LOCAL):
        occupied = (pos_s >> levels[j]) & 1
        above = changed >> levels[j]
        leave_c[j] = jnp.where((above >> 1) != 0, occupied, 0).astype(F32)

    block = LOCAL // 3
    halves[:, LOCAL * P_SIZE :, :] = jnp.zeros((seqs, P_SIZE, 2 * N), BF16)
    has_zero_in_a = level_0 == 0

    def gather_low(s, carry):
        load(s).wait()
        sums = []
        for part in range(3):
            total = None
            for j in range(part * block, (part + 1) * block):
                x = held[s, j * P_SIZE : (j + 1) * P_SIZE, :]
                high, low = split_two(x)
                halves[s, j * P_SIZE : (j + 1) * P_SIZE, 0:N] = high.astype(BF16)
                halves[s, j * P_SIZE : (j + 1) * P_SIZE, N : 2 * N] = low.astype(BF16)
                term = x * leave_c[j, pl.ds(s, 1), :]
                total = term if total is None else total + term
            sums.append(total)
        zero = jnp.zeros_like(sums[0])
        one_in_a, two_in_a = split > block, split > 2 * block
        in_a = sums[0] + jnp.where(one_in_a, sums[1], zero) + jnp.where(two_in_a, sums[2], zero)
        in_b = jnp.where(one_in_a, zero, sums[1]) + jnp.where(two_in_a, zero, sums[2])
        low_a[s] = in_a
        low_b[s] = in_b
        low_send[s] = jnp.where(has_zero_in_a, in_a, in_b).astype(BF16)
        return carry

    lax.fori_loop(0, seqs, gather_low, 0)

    taken_here = jnp.int32(0)
    for s in range(seqs):
        taken_here = taken_here + acc_ref[s]
    counts[sq] = jnp.full((8, 128), taken_here, jnp.int32).astype(F32)

    pl.semaphore_wait(barrier, expected)

    def remote(src, dst, send_sem, recv_sem, group, level):
        return pltpu.make_async_remote_copy(
            src_ref=src,
            dst_ref=dst,
            send_sem=send_sem,
            recv_sem=recv_sem,
            device_id=(group, level),
            device_id_type=MESH,
        )

    def y_copy(row):
        return remote(bc.at[slot], bc.at[slot], y_send.at[row], bc_recv.at[slot], sq, row * ROW + z)

    def z_copy(step):
        other = y * ROW + lax.rem(z + step, ROW)
        return remote(bc.at[slot], bc.at[slot], z_send.at[step], bc_recv.at[slot], sq, other)

    def x_copy(gap):
        target = wrapped(me - gap, devices)
        index = gap - X_LOW
        return remote(piece, xs.at[index], x_send.at[index], x_recv.at[index], sq, target)

    def low_copy():
        target = wrapped(me + 1, devices)
        return remote(low_send, low_recv, low_sems.at[0], low_sems.at[1], sq, target)

    def count_copy(step):
        return remote(
            counts.at[sq], counts.at[sq], n_send.at[step], n_recv.at[sq], lax.rem(sq + step, groups), me
        )

    def partial_copy(index, gap):
        target = wrapped(me + gap, devices)
        return remote(psend, pslots.at[index], p_send.at[index], p_recv.at[index], sq, target)

    sends_low = kind != 1
    gets_low = kind != 2
    gaps = [gap for gap in range(X_LOW, X_HIGH + 1) if gap != 0]
    near = (
        (0, 1, None, None),
        (1, 2, (kind == 0) | (kind == 3), (kind == 1) | (kind == 2)),
        (2, -1, kind == 3, kind == 2),
    )

    def when(cond, do):
        if cond is None:
            do()
        else:
            pl.when(cond)(do)

    @pl.when(is_source)
    def _():
        for row in range(columns - 1):
            y_copy(row).start()

    for gap in gaps:
        when(needs_values(wrapped(me - gap, devices), me), lambda: x_copy(gap).start())
    when(sends_low, lambda: low_copy().start())
    for step in range(1, groups):
        count_copy(step).start()

    head_lane = lax.broadcasted_iota(jnp.int32, (rows, H), 1)
    small[3].wait()
    small[4].wait()
    rates = rates_ref[...].reshape(rows, H)
    first_head = first_head_of(me)
    second_head = lax.rem(first_head + 1, H)
    row = lax.broadcasted_iota(jnp.int32, (rows, 128), 0)
    token = row & (K - 1)
    pos_rows = jnp.concatenate([jnp.full((K, 128), pos_ref[s], jnp.int32) for s in range(seqs)], 0)
    acc_rows = jnp.concatenate([jnp.full((K, 128), acc_ref[s], jnp.int32) for s in range(seqs)], 0)
    new_rows = pos_rows + acc_rows
    token_rows = pos_rows + token
    live = token < acc_rows

    def decays(head):
        rate = jnp.sum(jnp.where(head_lane == head, rates, 0.0), axis=1, keepdims=True)
        rate = jnp.broadcast_to(rate, (rows, 128))
        running = rate
        for by in (1, 2, 4):
            running = running + jnp.where(token >= by, pltpu.roll(running, by, 0), 0.0)
        cum = -running
        taken = -jnp.sum(jnp.where(live, rate, 0.0).reshape(seqs, K, 128), axis=1)
        taken_rows = jnp.broadcast_to(taken[:, None, :], (seqs, K, 128)).reshape(rows, 128)
        decay = jnp.where(live, jnp.exp(jnp.minimum(taken_rows - cum, 0.0)), 0.0)
        return cum, jnp.exp(cum), jnp.exp(taken), decay

    cum_a, grown_a, kept_a, decay_a = decays(first_head)
    cum_b, grown_b, kept_b, decay_b = decays(second_head)

    for j in range(LOCAL):
        in_a = j < split
        kept = jnp.where(in_a, kept_a, kept_b)
        occupied = (pos_s >> levels[j]) & 1
        new_occupied = (new_s >> levels[j]) & 1
        above = changed >> levels[j]
        stay_c[j] = jnp.where((above == 0) & (occupied == 1) & (new_occupied == 1), kept, 0.0)
        into_c[j] = jnp.where((above == 1) & (new_occupied == 1), kept, 0.0)

    weights = weights_ref[...].reshape(rows, LOCAL)
    local_lane = lax.broadcasted_iota(jnp.int32, (rows, LOCAL), 1)
    level_lane = lax.rem(level_0 + local_lane, L)
    weight_zero = jnp.sum(jnp.where(level_lane == 0, weights, 0.0), axis=1, keepdims=True)
    quads = (LOCAL + 1) // 2

    def of_lane(q):
        two = 2 * q + jnp.where(lower, 0, 1)
        return jnp.where(lower, levels[2 * q], levels[2 * q + 1]), two < split, two < LOCAL

    for q in range(quads):
        level, in_a, real = of_lane(q)
        first = jnp.broadcast_to(weights[:, 2 * q : 2 * q + 1], (rows, 128))
        if 2 * q + 1 < LOCAL:
            second = jnp.broadcast_to(weights[:, 2 * q + 1 : 2 * q + 2], (rows, 128))
        else:
            second = jnp.zeros((rows, 128), F32)
        occupied = ((pos_rows >> level) & 1) == 1
        grown = jnp.where(in_a, grown_a, grown_b)
        wide_w[q] = jnp.where(occupied & real, jnp.where(lower, first, second) * grown, 0.0)

    @pl.when(has_slot)
    def _():
        @pl.when(y != columns - 1)
        def _():
            remote(
                bc.at[slot], bc.at[slot], y_send.at[0], bc_recv.at[slot], sq, me
            ).wait_recv()

        for step in range(1, ROW):
            z_copy(step).start()

    for other in range(first_z, ROW):
        index = other - first_z

        @pl.when(z != other)
        def _():
            remote(
                bc.at[index], bc.at[index], y_send.at[0], bc_recv.at[index], sq, me
            ).wait_recv()

    got = [bc[i].astype(F32) for i in range(BC_SLOTS)]

    def vectors(first_feature):
        parts = []
        for r in range(2):
            part = jnp.zeros((half_rows, 128), F32)
            for i in range(BC_SLOTS):
                start = OWN_IN * (BC_FIRST + i) - first_feature
                if start > -OWN_IN and start < N:
                    moved = got[i]
                    by = (start - P_SIZE * r) % 128
                    if by:
                        moved = pltpu.roll(moved, by, 1)
                    part = jnp.where((half_lane >= start) & (half_lane < start + OWN_IN), moved, part)
            parts.append(part)
        return jnp.concatenate(parts, axis=0)

    in_vecs = vectors(H * P_SIZE)
    out_vecs = vectors(H * P_SIZE + N)
    c3 = out_vecs.reshape(seqs, K, N)
    c3 = jnp.concatenate([c3, jnp.zeros_like(c3)], axis=1).astype(BF16)
    cc[:, :, 0:N] = c3
    cc[:, :, N : 2 * N] = c3

    for gap in gaps:
        index = gap - X_LOW
        source = wrapped(me + gap, devices)
        when(
            needs_values(me, source),
            lambda: remote(
                piece, xs.at[index], x_send.at[index], x_recv.at[index], sq, me
            ).wait_recv(),
        )
    value_parts = []
    for r in range(2):
        part = jnp.zeros((half_rows, 128), F32)
        for gap in range(X_LOW, X_HIGH + 1):
            source = wrapped(me + gap, devices)
            start = value_offset(me, source)
            end = start + jnp.minimum(OWN_IN, H * P_SIZE - OWN_IN * source)
            wanted = needs_values(me, source)
            first = jnp.where(wanted, start, 128)
            by = lax.rem(start + 4 * H * P_SIZE - P_SIZE * r, 128)
            moved = pltpu.roll(xs[gap - X_LOW].astype(F32), by, 1)
            part = jnp.where((half_lane >= first) & (half_lane < end), moved, part)
        value_parts.append(part)
    values = jnp.concatenate(value_parts, axis=0)

    b16 = in_vecs.astype(BF16)
    scores = lax.dot_general(
        out_vecs.astype(BF16),
        jnp.concatenate([b16, b16], axis=0),
        (((1,), (1,)), ((), ())),
        preferred_element_type=F32,
    )
    cum_zero = jnp.where(has_zero_in_a, cum_a, cum_b)
    source_row = lane & (rows - 1)
    cum_across = jnp.sum(jnp.where(source_row == row, cum_zero, 0.0), axis=0, keepdims=True)
    before = ((source_row >> 3) == (row >> 3)) & (source_row <= row)
    mixing = jnp.where(before, jnp.exp(jnp.minimum(cum_zero - cum_across, 0.0)), 0.0) * scores
    high, low = split_two(mixing)
    v16 = values.astype(BF16)
    mixed = jnp.dot(
        jnp.where(lower, high, low).astype(BF16),
        jnp.concatenate([v16, v16], axis=0),
        preferred_element_type=F32,
    )
    zero_here = jnp.where(lower, 1, 0) == as_int(has_zero_in_a)
    psend[...] = jnp.where(zero_here, mixed * weight_zero, 0.0)

    lane8 = lane[:K]
    lower8 = lane8 < P_SIZE

    def read_out(s, carry):
        read = lax.dot_general(
            cc[s], halves[s], (((1,), (1,)), ((), ())), preferred_element_type=F32
        )
        sum_a = jnp.zeros((K, 128), F32)
        sum_b = jnp.zeros((K, 128), F32)
        at = pl.ds(pl.multiple_of(s * K, K), K)
        for q in range(quads):
            two = 2 * q + jnp.where(lower8, 0, 1)
            term = read[:K, q * 128 : (q + 1) * 128] * wide_w[q, at, :]
            sum_a = sum_a + jnp.where(two < split, term, 0.0)
            sum_b = sum_b + jnp.where(two < split, 0.0, term)
        sum_a = sum_a + pltpu.roll(sum_a, P_SIZE, 1)
        sum_b = sum_b + pltpu.roll(sum_b, P_SIZE, 1)
        psend[at, :] = psend[at, :] + jnp.where(lower8, sum_a, sum_b)
        return carry

    lax.fori_loop(0, seqs, read_out, 0)

    for index, gap, sends, _ in near:
        when(sends, lambda: partial_copy(index, gap).start())

    turned = pltpu.roll(values, P_SIZE, 1)
    values_a = jnp.where(lower, values, turned) * decay_a
    values_b = jnp.where(lower, turned, values) * decay_b
    b3 = in_vecs.reshape(seqs, K, N)
    bb[...] = jnp.concatenate([b3, b3], axis=1).astype(BF16)
    for q in range(quads):
        level, in_a, real = of_lane(q)
        until = new_rows >> level
        inside = ((until & 1) == 1) & ((token_rows >> level) + 1 == until) & live & real
        term = jnp.where(inside, jnp.where(in_a, values_a, values_b), 0.0)
        high, low = split_two(term)
        both = jnp.concatenate(
            [high.reshape(seqs, K, 128), low.reshape(seqs, K, 128)], axis=1
        )
        xg[:, :, q * 128 : (q + 1) * 128] = both.astype(BF16)

    when(gets_low, lambda: low_copy().wait_recv())

    def update(s, carry):
        tokens = lax.dot_general(
            xg[s], bb[s], (((0,), (0,)), ((), ())), preferred_element_type=F32
        )
        came = jnp.where(gets_low, low_recv[s].astype(F32), 0.0)
        merged_a = low_a[s] + came
        merged_b = low_b[s]
        merged = (
            merged_a,
            jnp.where(split > block, merged_a, merged_b),
            jnp.where(split > 2 * block, merged_a, merged_b),
        )
        for j in range(LOCAL):
            at = slice(j * P_SIZE, (j + 1) * P_SIZE)
            new_ref[s, at, :] = (
                held[s, at, :] * stay_c[j, pl.ds(s, 1), :]
                + merged[j // block] * into_c[j, pl.ds(s, 1), :]
                + tokens[at, :]
            )
        return carry

    lax.fori_loop(0, seqs, update, 0)

    for index, gap, _, gets in near:
        when(
            gets,
            lambda: remote(
                psend, pslots.at[index], p_send.at[index], p_recv.at[index], sq, me
            ).wait_recv(),
        )
    total = jnp.zeros((rows, 128), F32)
    sources = [(None, 0, None)] + [(index, -gap, gets) for index, gap, _, gets in near]
    for index, gap, gets in sources:
        source = wrapped(me + gap, devices)
        offset = OWN_OUT * me - P_SIZE * first_head_of(source)
        offset = jnp.where(offset < -(H * P_SIZE) // 2, offset + H * P_SIZE, offset)
        offset = jnp.where(offset > (H * P_SIZE) // 2, offset - H * P_SIZE, offset)
        by = lax.rem(4 * H * P_SIZE - offset, 128)
        end = P_SIZE * heads_of(source)
        if gets is not None:
            end = jnp.where(gets, end, -(1 << 20))
        moved = pltpu.roll(psend[...] if index is None else pslots[index], by, 1)
        total = total + jnp.where((lane + offset >= 0) & (lane + offset < end), moved, 0.0)
    out_ref[...] = total.reshape(seqs, K, 128)[:, :, 0:OWN_OUT].astype(BF16)

    for step in range(1, groups):
        other = lax.rem(sq + step, groups)
        remote(
            counts.at[other], counts.at[other], n_send.at[step], n_recv.at[other], sq, me
        ).wait_recv()
    taken = jnp.sum(counts[...], axis=0)
    share_ref[...] = taken[0:1, 0:1] / (groups * seqs * K)

    @pl.when(is_source)
    def _():
        for r in range(columns - 1):
            y_copy(r).wait_send()

    @pl.when(has_slot)
    def _():
        for step in range(1, ROW):
            z_copy(step).wait_send()

    for gap in gaps:
        when(needs_values(wrapped(me - gap, devices), me), lambda: x_copy(gap).wait_send())
    when(sends_low, lambda: low_copy().wait_send())
    for step in range(1, groups):
        count_copy(step).wait_send()
    for index, gap, sends, _ in near:
        when(sends, lambda: partial_copy(index, gap).wait_send())


def on_device(states, xbc, rates, level_weights, positions, accepted):
    devices = lax.axis_size("level")
    groups = lax.axis_size("seq")
    seqs = states.shape[0]
    rows = seqs * K
    wide = LOCAL * P_SIZE
    padded_wide = (LOCAL + 1) * P_SIZE
    vmem = pl.BlockSpec(memory_space=pltpu.VMEM)
    in_hbm = pl.BlockSpec(memory_space=pltpu.HBM)
    dma = pltpu.SemaphoreType.DMA
    x_slots = X_HIGH - X_LOW + 1
    outputs, new_states, share = pl.pallas_call(
        functools.partial(kernel, devices, groups),
        out_shape=(
            jax.ShapeDtypeStruct((seqs, K, OWN_OUT), BF16),
            jax.ShapeDtypeStruct((seqs, wide, N), F32),
            jax.ShapeDtypeStruct((1, 1), F32),
        ),
        in_specs=[in_hbm] * 6,
        out_specs=(vmem, vmem, vmem),
        scratch_shapes=[
            pltpu.VMEM(xbc.shape, BF16),
            pltpu.VMEM(rates.shape, F32),
            pltpu.VMEM(level_weights.shape, F32),
            pltpu.SMEM(positions.shape, jnp.int32),
            pltpu.SMEM(accepted.shape, jnp.int32),
            pltpu.VMEM((seqs, wide, N), F32),
            pltpu.VMEM((seqs, padded_wide, 2 * N), BF16),
            pltpu.VMEM((rows, 128), F32),
            pltpu.VMEM((rows // 2, 128), BF16),
            pltpu.VMEM((BC_SLOTS, rows // 2, 128), BF16),
            pltpu.VMEM((x_slots, rows // 2, 128), BF16),
            pltpu.VMEM((seqs, P_SIZE, N), BF16),
            pltpu.VMEM((seqs, P_SIZE, N), BF16),
            pltpu.VMEM((seqs, P_SIZE, N), F32),
            pltpu.VMEM((seqs, P_SIZE, N), F32),
            pltpu.VMEM((LOCAL, seqs, 128), F32),
            pltpu.VMEM((LOCAL, seqs, 128), F32),
            pltpu.VMEM((LOCAL, seqs, 128), F32),
            pltpu.VMEM(((LOCAL + 1) // 2, rows, 128), F32),
            pltpu.VMEM((seqs, 2 * K, 2 * N), BF16),
            pltpu.VMEM((seqs, 2 * K, N), BF16),
            pltpu.VMEM((seqs, 2 * K, padded_wide), BF16),
            pltpu.VMEM((rows, 128), F32),
            pltpu.VMEM((3, rows, 128), F32),
            pltpu.VMEM((groups, 8, 128), F32),
            dma((5,)),
            dma((seqs,)),
            dma((devices // ROW,)),
            dma((ROW,)),
            dma((x_slots,)),
            dma((BC_SLOTS,)),
            dma((x_slots,)),
            dma((2,)),
            dma((3,)),
            dma((3,)),
            dma((groups,)),
            dma((groups,)),
        ],
        compiler_params=pltpu.CompilerParams(
            collective_id=0, has_side_effects=True, vmem_limit_bytes=40 << 20
        ),
    )(
        *[
            pltpu.with_memory_space_constraint(x, pltpu.HBM)
            for x in (
                states.reshape(seqs, wide, N),
                xbc,
                rates,
                level_weights,
                positions,
                accepted,
            )
        ]
    )
    return outputs, new_states.reshape(states.shape), share.reshape(())


def solution(mesh):
    in_specs = (
        P("seq", "level", None, None),
        P("seq", None, "level"),
        P("seq", None, None),
        P("seq", None, "level"),
        P("seq"),
        P("seq"),
    )
    out_specs = (P("seq", None, "level"), P("seq", "level", None, None), P())
    return jax.shard_map(
        on_device, mesh=mesh, in_specs=in_specs, out_specs=out_specs, check_vma=False
    )
```

```python
import functools

import jax
import jax.numpy as jnp
from jax import lax
from jax.experimental import pallas as pl
from jax.experimental.pallas import tpu as pltpu
from jax.sharding import PartitionSpec as P

H = 24
P_SIZE = 64
N = 128
L = 20
K = 8
ROW = 8
OWN_IN = 56
OWN_OUT = 48
LOCAL = 15
BC_FIRST = 27
BC_SLOTS = 5
X_LOW, X_HIGH = -5, 2
MESH = pl.DeviceIdType.MESH
F32 = jnp.float32
BF16 = jnp.bfloat16


def first_head_of(d):
    return lax.rem(lax.div(LOCAL * d + L // 2, L), H)


def first_level_of(d):
    return lax.rem(LOCAL * d + L // 2, L)


def heads_of(d):
    return jnp.where(first_level_of(d) + LOCAL > L, 2, 1)


def value_offset(d, s):
    u = OWN_IN * s - P_SIZE * first_head_of(d)
    return jnp.where(u < -(H * P_SIZE) // 2, u + H * P_SIZE, u)


def needs_values(d, s):
    u = value_offset(d, s)
    return (s <= BC_FIRST) & (u > -OWN_IN) & (u < P_SIZE * heads_of(d))


def wrapped(d, devices):
    return lax.rem(d + devices, devices)


def as_int(x):
    return x.astype(jnp.int32)


def split_two(x):
    high = x.astype(BF16).astype(F32)
    return high, x - high


def kernel(
    devices,
    groups,
    states_ref,
    xbc_in,
    rates_in,
    weights_in,
    pos_in,
    acc_in,
    out_ref,
    new_ref,
    share_ref,
    xbc_ref,
    rates_ref,
    weights_ref,
    pos_ref,
    acc_ref,
    held,
    halves,
    padded,
    piece,
    bc,
    xs,
    low_send,
    low_recv,
    low_a,
    low_b,
    leave_c,
    stay_c,
    into_c,
    wide_w,
    parts,
    cc,
    bb,
    xg,
    psend,
    pslots,
    counts,
    small_sem,
    in_sem,
    y_send,
    z_send,
    x_send,
    bc_recv,
    x_recv,
    low_sems,
    p_send,
    p_recv,
    n_send,
    n_recv,
):
    seqs = xbc_ref.shape[0]
    rows = seqs * K
    me = lax.axis_index("level")
    sq = lax.axis_index("seq")
    y, z = lax.div(me, ROW), lax.rem(me, ROW)
    columns = devices // ROW
    first_z = BC_FIRST - (columns - 1) * ROW
    has_slot = z >= first_z
    is_source = has_slot & (y == columns - 1)
    kind = lax.rem(me, 4)
    slot = jnp.maximum(z - first_z, 0)

    small = [
        pltpu.make_async_copy(src, dst, small_sem.at[i])
        for i, (src, dst) in enumerate(
            (
                (xbc_in, xbc_ref),
                (pos_in, pos_ref),
                (acc_in, acc_ref),
                (rates_in, rates_ref),
                (weights_in, weights_ref),
            )
        )
    ]

    def load(s):
        return pltpu.make_async_copy(states_ref.at[s], held.at[s], in_sem.at[s])

    for copy in small:
        copy.start()
    for s in range(seqs):
        load(s).start()

    barrier = pltpu.get_barrier_semaphore()

    def greet(group, level):
        pl.semaphore_signal(barrier, inc=1, device_id=(group, level), device_id_type=MESH)

    for other in range(first_z, ROW):

        @pl.when(z != other)
        def _():
            greet(sq, y * ROW + other)

    @pl.when(has_slot & (y != columns - 1))
    def _():
        greet(sq, (columns - 1) * ROW + z)

    for gap in range(X_LOW, X_HIGH + 1):
        if gap != 0:
            source = wrapped(me + gap, devices)

            @pl.when(needs_values(me, source))
            def _():
                greet(sq, source)

    greet(sq, wrapped(me - 1, devices))

    @pl.when((kind == 1) | (kind == 2))
    def _():
        greet(sq, wrapped(me - 2, devices))

    @pl.when(kind == 2)
    def _():
        greet(sq, wrapped(me + 1, devices))

    for step in range(1, groups):
        greet(lax.rem(sq + step, groups), me)

    expected = 7 * as_int(has_slot) + (columns - 1) * as_int(is_source) + groups
    for gap in range(X_LOW, X_HIGH + 1):
        if gap != 0:
            expected = expected + as_int(needs_values(wrapped(me - gap, devices), me))
    expected = expected + as_int((kind == 0) | (kind == 3)) + as_int(kind == 3)

    lane = lax.broadcasted_iota(jnp.int32, (rows, 128), 1)
    lower = lane < P_SIZE
    half_rows = rows // 2
    half_lane = lane[:half_rows]
    half_lower = half_lane < P_SIZE

    padded[...] = jnp.zeros_like(padded)
    small[0].wait()
    padded[:, 0:OWN_IN] = xbc_ref[...].astype(F32).reshape(rows, OWN_IN)
    wide = padded[...]
    packed = jnp.where(half_lower, wide[:half_rows], pltpu.roll(wide[half_rows:], P_SIZE, 1))
    packed = packed.astype(BF16)
    piece[...] = packed
    xs[-X_LOW] = packed

    @pl.when(is_source)
    def _():
        bc[slot] = packed

    small[1].wait()
    small[2].wait()
    sub = lax.broadcasted_iota(jnp.int32, (seqs, 128), 0)
    pos_s = jnp.zeros((seqs, 128), jnp.int32)
    acc_s = jnp.zeros((seqs, 128), jnp.int32)
    for s in range(seqs):
        pos_s = jnp.where(sub == s, pos_ref[s], pos_s)
        acc_s = jnp.where(sub == s, acc_ref[s], acc_s)
    new_s = pos_s + acc_s
    changed = pos_s ^ new_s
    level_0 = first_level_of(me)
    split = jnp.minimum(L - level_0, LOCAL)
    levels = [lax.rem(level_0 + j, L) for j in range(LOCAL)] + [0]
    block = LOCAL // 3
    one_in_a, two_in_a = split > block, split > 2 * block
    has_zero_in_a = level_0 == 0

    taken_here = jnp.int32(0)
    for s in range(seqs):
        taken_here = taken_here + acc_ref[s]
    counts[sq] = jnp.full((8, 128), taken_here, jnp.int32).astype(F32)

    pl.semaphore_wait(barrier, expected)

    def remote(src, dst, send_sem, recv_sem, group, level):
        return pltpu.make_async_remote_copy(
            src_ref=src,
            dst_ref=dst,
            send_sem=send_sem,
            recv_sem=recv_sem,
            device_id=(group, level),
            device_id_type=MESH,
        )

    def y_copy(row):
        return remote(bc.at[slot], bc.at[slot], y_send.at[row], bc_recv.at[slot], sq, row * ROW + z)

    def z_copy(step):
        other = y * ROW + lax.rem(z + step, ROW)
        return remote(bc.at[slot], bc.at[slot], z_send.at[step], bc_recv.at[slot], sq, other)

    def x_copy(gap):
        target = wrapped(me - gap, devices)
        index = gap - X_LOW
        return remote(piece, xs.at[index], x_send.at[index], x_recv.at[index], sq, target)

    def low_copy():
        target = wrapped(me + 1, devices)
        return remote(low_send, low_recv, low_sems.at[0], low_sems.at[1], sq, target)

    def count_copy(step):
        return remote(
            counts.at[sq], counts.at[sq], n_send.at[step], n_recv.at[sq], lax.rem(sq + step, groups), me
        )

    def partial_copy(index, gap):
        target = wrapped(me + gap, devices)
        return remote(psend.at[index], pslots.at[index], p_send.at[index], p_recv.at[index], sq, target)

    sends_low = kind != 1
    gets_low = kind != 2
    gaps = [gap for gap in range(X_LOW, X_HIGH + 1) if gap != 0]
    near = (
        (0, 2, (kind == 0) | (kind == 3), (kind == 1) | (kind == 2)),
        (1, 1, None, None),
        (2, -1, kind == 3, kind == 2),
    )

    def when(cond, do):
        if cond is None:
            do()
        else:
            pl.when(cond)(do)

    z_steps = (4, 3, 5, 2, 6, 1, 7)

    @pl.when(is_source)
    def _():
        for r in range(columns - 1):
            y_copy(r).start()
        for step in z_steps:
            z_copy(step).start()

    for gap in gaps:
        when(needs_values(wrapped(me - gap, devices), me), lambda: x_copy(gap).start())
    for step in range(1, groups):
        count_copy(step).start()


    for j in range(LOCAL):
        occupied = (pos_s >> levels[j]) & 1
        above = changed >> levels[j]
        leave_c[j] = jnp.where((above >> 1) != 0, occupied, 0).astype(F32)

    def gather_low(s, carry):
        load(s).wait()
        sums = []
        for part in range(3):
            total = None
            for j in range(part * block, (part + 1) * block):
                x = held[s, j * P_SIZE : (j + 1) * P_SIZE, :]
                high, low = split_two(x)
                halves[s, j * P_SIZE : (j + 1) * P_SIZE, 0:N] = high.astype(BF16)
                halves[s, j * P_SIZE : (j + 1) * P_SIZE, N : 2 * N] = low.astype(BF16)
                term = x * leave_c[j, pl.ds(s, 1), :]
                total = term if total is None else total + term
            sums.append(total)
        zero = jnp.zeros_like(sums[0])
        in_a = sums[0] + jnp.where(one_in_a, sums[1], zero) + jnp.where(two_in_a, sums[2], zero)
        in_b = jnp.where(one_in_a, zero, sums[1]) + jnp.where(two_in_a, zero, sums[2])
        low_a[s] = in_a
        low_b[s] = in_b
        low_send[s] = jnp.where(has_zero_in_a, in_a, in_b).astype(BF16)
        return carry

    lax.fori_loop(0, seqs, gather_low, 0)

    when(sends_low, lambda: low_copy().start())

    @pl.when(has_slot & (y != columns - 1))
    def _():
        remote(bc.at[slot], bc.at[slot], y_send.at[0], bc_recv.at[slot], sq, me).wait_recv()
        for step in z_steps:
            z_copy(step).start()

    head_lane = lax.broadcasted_iota(jnp.int32, (rows, H), 1)
    small[3].wait()
    small[4].wait()
    rates = rates_ref[...].reshape(rows, H)
    first_head = first_head_of(me)
    second_head = lax.rem(first_head + 1, H)
    row = lax.broadcasted_iota(jnp.int32, (rows, 128), 0)
    token = row & (K - 1)
    pos_rows = jnp.concatenate([jnp.full((K, 128), pos_ref[s], jnp.int32) for s in range(seqs)], 0)
    acc_rows = jnp.concatenate([jnp.full((K, 128), acc_ref[s], jnp.int32) for s in range(seqs)], 0)
    new_rows = pos_rows + acc_rows
    token_rows = pos_rows + token
    live = token < acc_rows

    def decays(head):
        rate = jnp.sum(jnp.where(head_lane == head, rates, 0.0), axis=1, keepdims=True)
        rate = jnp.broadcast_to(rate, (rows, 128))
        running = rate
        for by in (1, 2, 4):
            running = running + jnp.where(token >= by, pltpu.roll(running, by, 0), 0.0)
        cum = -running
        taken = -jnp.sum(jnp.where(live, rate, 0.0).reshape(seqs, K, 128), axis=1)
        taken_rows = jnp.broadcast_to(taken[:, None, :], (seqs, K, 128)).reshape(rows, 128)
        decay = jnp.where(live, jnp.exp(jnp.minimum(taken_rows - cum, 0.0)), 0.0)
        return cum, jnp.exp(cum), jnp.exp(taken), decay

    cum_a, grown_a, kept_a, decay_a = decays(first_head)
    cum_b, grown_b, kept_b, decay_b = decays(second_head)

    for j in range(LOCAL):
        in_a = j < split
        kept = jnp.where(in_a, kept_a, kept_b)
        occupied = (pos_s >> levels[j]) & 1
        new_occupied = (new_s >> levels[j]) & 1
        above = changed >> levels[j]
        stay_c[j] = jnp.where((above == 0) & (occupied == 1) & (new_occupied == 1), kept, 0.0)
        into_c[j] = jnp.where((above == 1) & (new_occupied == 1), kept, 0.0)

    weights = weights_ref[...].reshape(rows, LOCAL)
    local_lane = lax.broadcasted_iota(jnp.int32, (rows, LOCAL), 1)
    level_lane = lax.rem(level_0 + local_lane, L)
    weight_zero = jnp.sum(jnp.where(level_lane == 0, weights, 0.0), axis=1, keepdims=True)
    quads = (LOCAL + 1) // 2

    def of_lane(q):
        two = 2 * q + jnp.where(lower, 0, 1)
        return jnp.where(lower, levels[2 * q], levels[2 * q + 1]), two < split, two < LOCAL

    padded[:, 0:LOCAL] = weights
    here = lane < LOCAL
    level = level_0 + jnp.where(here, lane, 0)
    level = jnp.where(level >= L, level - L, level)
    shown = here & (((pos_rows >> level) & 1) == 1)
    by_token = jnp.where(shown, padded[...] * jnp.where(lane < split, grown_a, grown_b), 0.0)
    by_level = jnp.transpose(jnp.concatenate([by_token, jnp.zeros_like(by_token)], axis=0))
    by_level = by_level[: LOCAL + 1]
    for s in range(seqs):
        wide_w[s] = jnp.where((lane[: LOCAL + 1] >> 3) == s, by_level, 0.0)
    parts[...] = jnp.zeros_like(parts)

    for other in range(first_z, ROW):
        index = other - first_z

        @pl.when(z != other)
        def _():
            remote(
                bc.at[index], bc.at[index], y_send.at[0], bc_recv.at[index], sq, me
            ).wait_recv()

    got = [bc[i].astype(F32) for i in range(BC_SLOTS)]

    def vectors(first_feature):
        pair = []
        for r in range(2):
            part = jnp.zeros((half_rows, 128), F32)
            for i in range(BC_SLOTS):
                start = OWN_IN * (BC_FIRST + i) - first_feature
                if start > -OWN_IN and start < N:
                    moved = got[i]
                    by = (start - P_SIZE * r) % 128
                    if by:
                        moved = pltpu.roll(moved, by, 1)
                    part = jnp.where((half_lane >= start) & (half_lane < start + OWN_IN), moved, part)
            pair.append(part)
        return jnp.concatenate(pair, axis=0)

    in_vecs = vectors(H * P_SIZE)
    out_vecs = vectors(H * P_SIZE + N)
    across = jnp.transpose(jnp.concatenate([out_vecs, jnp.zeros_like(out_vecs)], axis=0))
    across = across.astype(BF16)
    cc[0:N, :] = across
    cc[N : 2 * N, :] = across

    for gap in gaps:
        index = gap - X_LOW
        source = wrapped(me + gap, devices)
        when(
            needs_values(me, source),
            lambda: remote(
                piece, xs.at[index], x_send.at[index], x_recv.at[index], sq, me
            ).wait_recv(),
        )
    value_parts = []
    for r in range(2):
        part = jnp.zeros((half_rows, 128), F32)
        for gap in range(X_LOW, X_HIGH + 1):
            source = wrapped(me + gap, devices)
            start = value_offset(me, source)
            end = start + jnp.minimum(OWN_IN, H * P_SIZE - OWN_IN * source)
            wanted = needs_values(me, source)
            first = jnp.where(wanted, start, 128)
            by = lax.rem(start + 4 * H * P_SIZE - P_SIZE * r, 128)
            moved = pltpu.roll(xs[gap - X_LOW].astype(F32), by, 1)
            part = jnp.where((half_lane >= first) & (half_lane < end), moved, part)
        value_parts.append(part)
    values = jnp.concatenate(value_parts, axis=0)

    b16 = in_vecs.astype(BF16)
    scores = lax.dot_general(
        out_vecs.astype(BF16),
        jnp.concatenate([b16, b16], axis=0),
        (((1,), (1,)), ((), ())),
        preferred_element_type=F32,
    )
    cum_zero = jnp.where(has_zero_in_a, cum_a, cum_b)
    source_row = lane & (rows - 1)
    cum_across = jnp.sum(jnp.where(source_row == row, cum_zero, 0.0), axis=0, keepdims=True)
    before = ((source_row >> 3) == (row >> 3)) & (source_row <= row)
    mixing = jnp.where(before, jnp.exp(jnp.minimum(cum_zero - cum_across, 0.0)), 0.0) * scores
    high, low = split_two(mixing)
    v16 = values.astype(BF16)
    mixed = jnp.dot(
        jnp.where(lower, high, low).astype(BF16),
        jnp.concatenate([v16, v16], axis=0),
        preferred_element_type=F32,
    )
    zero_here = jnp.where(lower, 1, 0) == as_int(has_zero_in_a)
    drafts = jnp.where(zero_here, mixed * weight_zero, 0.0)

    def read_out(s, carry):
        size = block * P_SIZE
        for part in range(3):
            read = jnp.dot(
                halves[s, part * size : (part + 1) * size, :], cc[...], preferred_element_type=F32
            )
            total = parts[part]
            for i in range(block):
                j = part * block + i
                total = total + read[i * P_SIZE : (i + 1) * P_SIZE, :] * wide_w[s, j : j + 1, :]
            parts[part] = total
        return carry

    lax.fori_loop(0, seqs, read_out, 0, unroll=2)

    zero = jnp.zeros((P_SIZE, 128), F32)
    in_a = parts[0] + jnp.where(one_in_a, parts[1], zero) + jnp.where(two_in_a, parts[2], zero)
    in_b = jnp.where(one_in_a, zero, parts[1]) + jnp.where(two_in_a, zero, parts[2])
    readout = jnp.transpose(jnp.concatenate([in_a, in_b], axis=0))[:rows]
    features = readout + drafts
    held_end = P_SIZE * heads_of(me)

    def packed_for(gap):
        offset = OWN_OUT * wrapped(me + gap, devices) - P_SIZE * first_head
        offset = jnp.where(offset < -(H * P_SIZE) // 2, offset + H * P_SIZE, offset)
        offset = jnp.where(offset > (H * P_SIZE) // 2, offset - H * P_SIZE, offset)
        moved = pltpu.roll(features, lax.rem(4 * H * P_SIZE - offset, 128), 1)
        wanted = (lane < OWN_OUT) & (lane + offset >= 0) & (lane + offset < held_end)
        moved = jnp.where(wanted, moved, 0.0)
        return moved[:half_rows] + pltpu.roll(moved[half_rows:], P_SIZE, 1)

    for index, gap, _, _ in near:
        psend[index] = packed_for(gap)
    for index, gap, sends, _ in near:
        when(sends, lambda: partial_copy(index, gap).start())
    own = packed_for(0)

    turned = pltpu.roll(values, P_SIZE, 1)
    values_a = jnp.where(lower, values, turned) * decay_a
    values_b = jnp.where(lower, turned, values) * decay_b
    b3 = in_vecs.reshape(seqs, K, N)
    bb[...] = jnp.concatenate([b3, b3], axis=1).astype(BF16)
    for q in range(quads):
        level, in_a, real = of_lane(q)
        until = new_rows >> level
        inside = ((until & 1) == 1) & ((token_rows >> level) + 1 == until) & live & real
        term = jnp.where(inside, jnp.where(in_a, values_a, values_b), 0.0)
        high, low = split_two(term)
        both = jnp.concatenate(
            [high.reshape(seqs, K, 128), low.reshape(seqs, K, 128)], axis=1
        )
        xg[:, :, q * 128 : (q + 1) * 128] = both.astype(BF16)

    when(gets_low, lambda: low_copy().wait_recv())

    def update(s, carry):
        tokens = lax.dot_general(
            xg[s], bb[s], (((0,), (0,)), ((), ())), preferred_element_type=F32
        )
        came = jnp.where(gets_low, low_recv[s].astype(F32), 0.0)
        merged_a = low_a[s] + came
        merged_b = low_b[s]
        merged = (
            merged_a,
            jnp.where(split > block, merged_a, merged_b),
            jnp.where(split > 2 * block, merged_a, merged_b),
        )
        for j in range(LOCAL):
            at = slice(j * P_SIZE, (j + 1) * P_SIZE)
            new_ref[s, at, :] = (
                held[s, at, :] * stay_c[j, pl.ds(s, 1), :]
                + merged[j // block] * into_c[j, pl.ds(s, 1), :]
                + tokens[at, :]
            )
        return carry

    lax.fori_loop(0, seqs, update, 0)

    for index, gap, _, gets in near:
        when(
            gets,
            lambda: remote(
                psend.at[index], pslots.at[index], p_send.at[index], p_recv.at[index], sq, me
            ).wait_recv(),
        )
    total = own
    for index, _, _, gets in near:
        came = pslots[index]
        total = total + (came if gets is None else jnp.where(gets, came, 0.0))
    total = jnp.concatenate([total, pltpu.roll(total, P_SIZE, 1)], axis=0)
    out_ref[...] = total.reshape(seqs, K, 128)[:, :, 0:OWN_OUT].astype(BF16)

    for step in range(1, groups):
        other = lax.rem(sq + step, groups)
        remote(
            counts.at[other], counts.at[other], n_send.at[step], n_recv.at[other], sq, me
        ).wait_recv()
    taken = jnp.sum(counts[...], axis=0)
    share_ref[...] = taken[0:1, 0:1] / (groups * seqs * K)

    @pl.when(is_source)
    def _():
        for r in range(columns - 1):
            y_copy(r).wait_send()

    @pl.when(has_slot)
    def _():
        for step in range(1, ROW):
            z_copy(step).wait_send()

    for gap in gaps:
        when(needs_values(wrapped(me - gap, devices), me), lambda: x_copy(gap).wait_send())
    when(sends_low, lambda: low_copy().wait_send())
    for step in range(1, groups):
        count_copy(step).wait_send()
    for index, gap, sends, _ in near:
        when(sends, lambda: partial_copy(index, gap).wait_send())


def flush(new_in, out_in, new_out, out_out, sems):
    pieces = new_in.shape[0]
    copies = [pltpu.make_async_copy(out_in, out_out, sems.at[pieces])]
    copies += [pltpu.make_async_copy(new_in.at[s], new_out.at[s], sems.at[s]) for s in range(pieces)]
    for copy in copies:
        copy.start()
    for copy in copies:
        copy.wait()


def on_device(states, xbc, rates, level_weights, positions, accepted):
    devices = lax.axis_size("level")
    groups = lax.axis_size("seq")
    seqs = states.shape[0]
    rows = seqs * K
    wide = LOCAL * P_SIZE
    padded_wide = (LOCAL + 1) * P_SIZE
    vmem = pl.BlockSpec(memory_space=pltpu.VMEM)
    in_hbm = pl.BlockSpec(memory_space=pltpu.HBM)
    dma = pltpu.SemaphoreType.DMA
    x_slots = X_HIGH - X_LOW + 1
    outputs, new_states, share = pl.pallas_call(
        functools.partial(kernel, devices, groups),
        out_shape=(
            jax.ShapeDtypeStruct((seqs, K, OWN_OUT), BF16),
            jax.ShapeDtypeStruct((seqs, wide, N), F32),
            jax.ShapeDtypeStruct((1, 1), F32),
        ),
        in_specs=[in_hbm] * 6,
        out_specs=(vmem, vmem, vmem),
        scratch_shapes=[
            pltpu.VMEM(xbc.shape, BF16),
            pltpu.VMEM(rates.shape, F32),
            pltpu.VMEM(level_weights.shape, F32),
            pltpu.SMEM(positions.shape, jnp.int32),
            pltpu.SMEM(accepted.shape, jnp.int32),
            pltpu.VMEM((seqs, wide, N), F32),
            pltpu.VMEM((seqs, wide, 2 * N), BF16),
            pltpu.VMEM((rows, 128), F32),
            pltpu.VMEM((rows // 2, 128), BF16),
            pltpu.VMEM((BC_SLOTS, rows // 2, 128), BF16),
            pltpu.VMEM((x_slots, rows // 2, 128), BF16),
            pltpu.VMEM((seqs, P_SIZE, N), BF16),
            pltpu.VMEM((seqs, P_SIZE, N), BF16),
            pltpu.VMEM((seqs, P_SIZE, N), F32),
            pltpu.VMEM((seqs, P_SIZE, N), F32),
            pltpu.VMEM((LOCAL, seqs, 128), F32),
            pltpu.VMEM((LOCAL, seqs, 128), F32),
            pltpu.VMEM((LOCAL, seqs, 128), F32),
            pltpu.VMEM((seqs, LOCAL + 1, 128), F32),
            pltpu.VMEM((3, P_SIZE, 128), F32),
            pltpu.VMEM((2 * N, 128), BF16),
            pltpu.VMEM((seqs, 2 * K, N), BF16),
            pltpu.VMEM((seqs, 2 * K, padded_wide), BF16),
            pltpu.VMEM((3, rows // 2, 128), F32),
            pltpu.VMEM((3, rows // 2, 128), F32),
            pltpu.VMEM((groups, 8, 128), F32),
            dma((5,)),
            dma((seqs,)),
            dma((devices // ROW,)),
            dma((ROW,)),
            dma((x_slots,)),
            dma((BC_SLOTS,)),
            dma((x_slots,)),
            dma((2,)),
            dma((3,)),
            dma((3,)),
            dma((groups,)),
            dma((groups,)),
        ],
        compiler_params=pltpu.CompilerParams(
            collective_id=0, has_side_effects=True, vmem_limit_bytes=40 << 20
        ),
    )(
        *[
            pltpu.with_memory_space_constraint(x, pltpu.HBM)
            for x in (
                states.reshape(seqs, wide, N),
                xbc,
                rates,
                level_weights,
                positions,
                accepted,
            )
        ]
    )
    anywhere = pl.BlockSpec(memory_space=pl.ANY)
    new_states, outputs = pl.pallas_call(
        flush,
        out_shape=(
            jax.ShapeDtypeStruct(new_states.shape, F32),
            jax.ShapeDtypeStruct(outputs.shape, BF16),
        ),
        in_specs=[anywhere, anywhere],
        out_specs=(in_hbm, in_hbm),
        scratch_shapes=[dma((seqs + 1,))],
        compiler_params=pltpu.CompilerParams(vmem_limit_bytes=4 << 20),
    )(new_states, outputs)
    return outputs, new_states.reshape(states.shape), share.reshape(())


def solution(mesh):
    in_specs = (
        P("seq", "level", None, None),
        P("seq", None, "level"),
        P("seq", None, None),
        P("seq", None, "level"),
        P("seq"),
        P("seq"),
    )
    out_specs = (P("seq", None, "level"), P("seq", "level", None, None), P())
    return jax.shard_map(
        on_device, mesh=mesh, in_specs=in_specs, out_specs=out_specs, check_vma=False
    )
```

```python
import functools

import jax
import jax.numpy as jnp
from jax import lax
from jax.experimental import pallas as pl
from jax.experimental.pallas import tpu as pltpu
from jax.sharding import PartitionSpec as P

H = 24
P_SIZE = 64
N = 128
L = 20
K = 8
ROW = 8
OWN_IN = 56
OWN_OUT = 48
LOCAL = 15
BC_FIRST = 27
BC_SLOTS = 5
LATE = 4
X_LOW, X_HIGH = -5, 2
MESH = pl.DeviceIdType.MESH
F32 = jnp.float32
BF16 = jnp.bfloat16


def first_head_of(d):
    return lax.rem(lax.div(LOCAL * d + L // 2, L), H)


def first_level_of(d):
    return lax.rem(LOCAL * d + L // 2, L)


def heads_of(d):
    return jnp.where(first_level_of(d) + LOCAL > L, 2, 1)


def value_offset(d, s):
    u = OWN_IN * s - P_SIZE * first_head_of(d)
    return jnp.where(u < -(H * P_SIZE) // 2, u + H * P_SIZE, u)


def needs_values(d, s):
    u = value_offset(d, s)
    return (s <= BC_FIRST) & (u > -OWN_IN) & (u < P_SIZE * heads_of(d))


def wrapped(d, devices):
    return lax.rem(d + devices, devices)


def as_int(x):
    return x.astype(jnp.int32)


def split_two(x):
    high = x.astype(BF16).astype(F32)
    return high, x - high


def kernel(
    devices,
    groups,
    states_ref,
    xbc_in,
    rates_in,
    weights_in,
    pos_in,
    acc_in,
    out_ref,
    new_ref,
    share_ref,
    xbc_ref,
    rates_ref,
    weights_ref,
    pos_ref,
    acc_ref,
    held,
    halves,
    padded,
    piece,
    bc,
    xs,
    low_send,
    low_recv,
    low_a,
    low_b,
    leave_c,
    stay_c,
    into_c,
    wide_w,
    parts,
    cc,
    bb,
    xg,
    psend,
    pslots,
    counts,
    shared,
    small_sem,
    in_sem,
    y_send,
    z_send,
    x_send,
    bc_recv,
    x_recv,
    low_sems,
    p_send,
    p_recv,
    n_send,
    n_recv,
    late_send,
    t_send,
    t_recv,
):
    seqs = xbc_ref.shape[0]
    rows = seqs * K
    me = lax.axis_index("level")
    sq = lax.axis_index("seq")
    y, z = lax.div(me, ROW), lax.rem(me, ROW)
    columns = devices // ROW
    first_z = BC_FIRST - (columns - 1) * ROW
    has_slot = z >= first_z
    is_source = has_slot & (y == columns - 1)
    is_late = (y == columns - 1) & (z == LATE)
    feeds_late = (y == 0) & (z == LATE)
    is_root = me == 0
    kind = lax.rem(me, 4)
    slot = jnp.maximum(z - first_z, 0)

    small = [
        pltpu.make_async_copy(src, dst, small_sem.at[i])
        for i, (src, dst) in enumerate(
            (
                (xbc_in, xbc_ref),
                (pos_in, pos_ref),
                (acc_in, acc_ref),
                (rates_in, rates_ref),
                (weights_in, weights_ref),
            )
        )
    ]

    def load(s):
        return pltpu.make_async_copy(states_ref.at[s], held.at[s], in_sem.at[s])

    for copy in small:
        copy.start()
    for s in range(seqs):
        load(s).start()

    barrier = pltpu.get_barrier_semaphore()

    def greet(group, level):
        pl.semaphore_signal(barrier, inc=1, device_id=(group, level), device_id_type=MESH)

    for other in range(first_z, ROW):

        @pl.when((z != other) & ((y != columns - 1) | (z != LATE) | (other == LATE)))
        def _():
            greet(sq, y * ROW + other)

    @pl.when(is_late)
    def _():
        greet(sq, LATE)

    @pl.when(has_slot & (y != columns - 1))
    def _():
        greet(sq, (columns - 1) * ROW + z)

    for gap in range(X_LOW, X_HIGH + 1):
        if gap != 0:
            source = wrapped(me + gap, devices)

            @pl.when(needs_values(me, source))
            def _():
                greet(sq, source)

    greet(sq, wrapped(me - 1, devices))

    @pl.when((kind == 1) | (kind == 2))
    def _():
        greet(sq, wrapped(me - 2, devices))

    @pl.when(kind == 2)
    def _():
        greet(sq, wrapped(me + 1, devices))

    @pl.when(is_root)
    def _():
        for step in range(1, groups):
            greet(lax.rem(sq + step, groups), me)

    @pl.when(me != 0)
    def _():
        greet(sq, 0)

    expected = (ROW - 1) * as_int(has_slot) + (columns - 1) * as_int(is_source) + 1
    expected = expected - as_int(is_source & (z != LATE)) + as_int(feeds_late)
    expected = expected + (devices + groups - 2) * as_int(is_root)
    for gap in range(X_LOW, X_HIGH + 1):
        if gap != 0:
            expected = expected + as_int(needs_values(wrapped(me - gap, devices), me))
    expected = expected + as_int((kind == 0) | (kind == 3)) + as_int(kind == 3)

    lane = lax.broadcasted_iota(jnp.int32, (rows, 128), 1)
    lower = lane < P_SIZE
    half_rows = rows // 2
    half_lane = lane[:half_rows]
    half_lower = half_lane < P_SIZE

    padded[...] = jnp.zeros_like(padded)
    small[0].wait()
    padded[:, 0:OWN_IN] = xbc_ref[...].astype(F32).reshape(rows, OWN_IN)
    wide = padded[...]
    packed = jnp.where(half_lower, wide[:half_rows], pltpu.roll(wide[half_rows:], P_SIZE, 1))
    packed = packed.astype(BF16)
    piece[...] = packed
    xs[-X_LOW] = packed

    @pl.when(is_source)
    def _():
        bc[slot] = packed

    small[1].wait()
    small[2].wait()
    sub = lax.broadcasted_iota(jnp.int32, (seqs, 128), 0)
    pos_s = jnp.zeros((seqs, 128), jnp.int32)
    acc_s = jnp.zeros((seqs, 128), jnp.int32)
    for s in range(seqs):
        pos_s = jnp.where(sub == s, pos_ref[s], pos_s)
        acc_s = jnp.where(sub == s, acc_ref[s], acc_s)
    new_s = pos_s + acc_s
    changed = pos_s ^ new_s
    level_0 = first_level_of(me)
    split = jnp.minimum(L - level_0, LOCAL)
    levels = [lax.rem(level_0 + j, L) for j in range(LOCAL)] + [0]
    block = LOCAL // 3
    one_in_a, two_in_a = split > block, split > 2 * block
    has_zero_in_a = level_0 == 0

    for j in range(LOCAL):
        occupied = (pos_s >> levels[j]) & 1
        above = changed >> levels[j]
        leave_c[j] = jnp.where((above >> 1) != 0, occupied, 0).astype(F32)

    def gather_low(s, carry):
        load(s).wait()
        sums = []
        for part in range(3):
            total = None
            for j in range(part * block, (part + 1) * block):
                x = held[s, j * P_SIZE : (j + 1) * P_SIZE, :]
                high, low = split_two(x)
                halves[s, j * P_SIZE : (j + 1) * P_SIZE, 0:N] = high.astype(BF16)
                halves[s, j * P_SIZE : (j + 1) * P_SIZE, N : 2 * N] = low.astype(BF16)
                term = x * leave_c[j, pl.ds(s, 1), :]
                total = term if total is None else total + term
            sums.append(total)
        zero = jnp.zeros_like(sums[0])
        in_a = sums[0] + jnp.where(one_in_a, sums[1], zero) + jnp.where(two_in_a, sums[2], zero)
        in_b = jnp.where(one_in_a, zero, sums[1]) + jnp.where(two_in_a, zero, sums[2])
        low_a[s] = in_a
        low_b[s] = in_b
        low_send[s] = jnp.where(has_zero_in_a, in_a, in_b).astype(BF16)
        return carry

    @pl.when(z < first_z)
    def _():
        lax.fori_loop(0, seqs, gather_low, 0)

    @pl.when(is_root)
    def _():
        taken_here = jnp.int32(0)
        for s in range(seqs):
            taken_here = taken_here + acc_ref[s]
        counts[sq] = jnp.full((8, 128), taken_here, jnp.int32).astype(F32)

    pl.semaphore_wait(barrier, expected)

    def remote(src, dst, send_sem, recv_sem, group, level):
        return pltpu.make_async_remote_copy(
            src_ref=src,
            dst_ref=dst,
            send_sem=send_sem,
            recv_sem=recv_sem,
            device_id=(group, level),
            device_id_type=MESH,
        )

    def y_copy(row):
        return remote(bc.at[slot], bc.at[slot], y_send.at[row], bc_recv.at[slot], sq, row * ROW + z)

    def z_copy(step):
        other = y * ROW + lax.rem(z + step, ROW)
        return remote(bc.at[slot], bc.at[slot], z_send.at[step], bc_recv.at[slot], sq, other)

    def x_copy(gap):
        target = wrapped(me - gap, devices)
        index = gap - X_LOW
        return remote(piece, xs.at[index], x_send.at[index], x_recv.at[index], sq, target)

    def low_copy():
        target = wrapped(me + 1, devices)
        return remote(low_send, low_recv, low_sems.at[0], low_sems.at[1], sq, target)

    def count_copy(step):
        return remote(
            counts.at[sq], counts.at[sq], n_send.at[step], n_recv.at[sq], lax.rem(sq + step, groups), me
        )

    others = [index for index in range(BC_SLOTS) if index != LATE - first_z]

    def late_copy(index):
        target = (columns - 1) * ROW + LATE
        return remote(bc.at[index], bc.at[index], late_send.at[index], bc_recv.at[index], sq, target)

    def total_copy(step):
        return remote(shared, shared, t_send.at[step], t_recv.at[0], sq, step)

    def partial_copy(index, gap):
        target = wrapped(me + gap, devices)
        return remote(psend.at[index], pslots.at[index], p_send.at[index], p_recv.at[index], sq, target)

    sends_low = kind != 1
    gets_low = kind != 2
    gaps = [gap for gap in range(X_LOW, X_HIGH + 1) if gap != 0]
    near = (
        (0, 2, (kind == 0) | (kind == 3), (kind == 1) | (kind == 2)),
        (1, 1, None, None),
        (2, -1, kind == 3, kind == 2),
    )

    def when(cond, do):
        if cond is None:
            do()
        else:
            pl.when(cond)(do)

    z_steps = (4, 3, 5, 2, 6, 1, 7)

    @pl.when(is_source)
    def _():
        for r in range(columns - 1):
            y_copy(r).start()
        for step in z_steps:
            when(lax.rem(z + step, ROW) != LATE, lambda: z_copy(step).start())

    for gap in gaps:
        when(needs_values(wrapped(me - gap, devices), me), lambda: x_copy(gap).start())
    @pl.when(is_root)
    def _():
        for step in range(1, groups):
            count_copy(step).start()


    @pl.when(has_slot)
    def _():
        lax.fori_loop(0, seqs, gather_low, 0)

    when(sends_low, lambda: low_copy().start())

    @pl.when(has_slot & (y != columns - 1))
    def _():
        remote(bc.at[slot], bc.at[slot], y_send.at[0], bc_recv.at[slot], sq, me).wait_recv()
        for step in z_steps:
            z_copy(step).start()

    head_lane = lax.broadcasted_iota(jnp.int32, (rows, H), 1)
    small[3].wait()
    small[4].wait()
    rates = rates_ref[...].reshape(rows, H)
    first_head = first_head_of(me)
    second_head = lax.rem(first_head + 1, H)
    row = lax.broadcasted_iota(jnp.int32, (rows, 128), 0)
    token = row & (K - 1)
    pos_rows = jnp.concatenate([jnp.full((K, 128), pos_ref[s], jnp.int32) for s in range(seqs)], 0)
    acc_rows = jnp.concatenate([jnp.full((K, 128), acc_ref[s], jnp.int32) for s in range(seqs)], 0)
    new_rows = pos_rows + acc_rows
    token_rows = pos_rows + token
    live = token < acc_rows

    def decays(head):
        rate = jnp.sum(jnp.where(head_lane == head, rates, 0.0), axis=1, keepdims=True)
        rate = jnp.broadcast_to(rate, (rows, 128))
        running = rate
        for by in (1, 2, 4):
            running = running + jnp.where(token >= by, pltpu.roll(running, by, 0), 0.0)
        cum = -running
        taken = -jnp.sum(jnp.where(live, rate, 0.0).reshape(seqs, K, 128), axis=1)
        taken_rows = jnp.broadcast_to(taken[:, None, :], (seqs, K, 128)).reshape(rows, 128)
        decay = jnp.where(live, jnp.exp(jnp.minimum(taken_rows - cum, 0.0)), 0.0)
        return cum, jnp.exp(cum), jnp.exp(taken), decay

    cum_a, grown_a, kept_a, decay_a = decays(first_head)
    cum_b, grown_b, kept_b, decay_b = decays(second_head)

    for j in range(LOCAL):
        in_a = j < split
        kept = jnp.where(in_a, kept_a, kept_b)
        occupied = (pos_s >> levels[j]) & 1
        new_occupied = (new_s >> levels[j]) & 1
        above = changed >> levels[j]
        stay_c[j] = jnp.where((above == 0) & (occupied == 1) & (new_occupied == 1), kept, 0.0)
        into_c[j] = jnp.where((above == 1) & (new_occupied == 1), kept, 0.0)

    weights = weights_ref[...].reshape(rows, LOCAL)
    local_lane = lax.broadcasted_iota(jnp.int32, (rows, LOCAL), 1)
    level_lane = lax.rem(level_0 + local_lane, L)
    weight_zero = jnp.sum(jnp.where(level_lane == 0, weights, 0.0), axis=1, keepdims=True)
    quads = (LOCAL + 1) // 2

    def of_lane(q):
        two = 2 * q + jnp.where(lower, 0, 1)
        return jnp.where(lower, levels[2 * q], levels[2 * q + 1]), two < split, two < LOCAL

    padded[:, 0:LOCAL] = weights
    here = lane < LOCAL
    level = level_0 + jnp.where(here, lane, 0)
    level = jnp.where(level >= L, level - L, level)
    shown = here & (((pos_rows >> level) & 1) == 1)
    by_token = jnp.where(shown, padded[...] * jnp.where(lane < split, grown_a, grown_b), 0.0)
    by_level = jnp.transpose(jnp.concatenate([by_token, jnp.zeros_like(by_token)], axis=0))
    by_level = by_level[: LOCAL + 1]
    for s in range(seqs):
        wide_w[s] = jnp.where((lane[: LOCAL + 1] >> 3) == s, by_level, 0.0)
    parts[...] = jnp.zeros_like(parts)

    @pl.when(is_root)
    def _():
        for step in range(1, groups):
            other = lax.rem(sq + step, groups)
            remote(
                counts.at[other], counts.at[other], n_send.at[step], n_recv.at[other], sq, me
            ).wait_recv()
        shared[...] = jnp.sum(counts[...], axis=0)
        for step in range(1, devices):
            total_copy(step).start()

    def await_pieces(indices):
        for index in indices:

            @pl.when(z != first_z + index)
            def _():
                remote(
                    bc.at[index], bc.at[index], y_send.at[0], bc_recv.at[index], sq, me
                ).wait_recv()

        for index in indices:
            if index in others:

                @pl.when(feeds_late)
                def _():
                    late_copy(index).start()

    def vectors(first_feature, indices):
        pair = []
        got = [bc[i].astype(F32) for i in indices]
        for r in range(2):
            part = jnp.zeros((half_rows, 128), F32)
            for i, moved in zip(indices, got):
                start = OWN_IN * (BC_FIRST + i) - first_feature
                by = (start - P_SIZE * r) % 128
                if by:
                    moved = pltpu.roll(moved, by, 1)
                part = jnp.where((half_lane >= start) & (half_lane < start + OWN_IN), moved, part)
            pair.append(part)
        return jnp.concatenate(pair, axis=0)

    await_pieces((2, 3, 4))
    out_vecs = vectors(H * P_SIZE + N, (2, 3, 4))
    across = jnp.transpose(jnp.concatenate([out_vecs, jnp.zeros_like(out_vecs)], axis=0))
    across = across.astype(BF16)
    cc[0:N, :] = across
    cc[N : 2 * N, :] = across

    def read_out(s, carry):
        size = block * P_SIZE
        for part in range(3):
            read = jnp.dot(
                halves[s, part * size : (part + 1) * size, :], cc[...], preferred_element_type=F32
            )
            total = parts[part]
            for i in range(block):
                j = part * block + i
                total = total + read[i * P_SIZE : (i + 1) * P_SIZE, :] * wide_w[s, j : j + 1, :]
            parts[part] = total
        return carry

    lax.fori_loop(0, seqs, read_out, 0, unroll=2)

    zero = jnp.zeros((P_SIZE, 128), F32)
    in_a = parts[0] + jnp.where(one_in_a, parts[1], zero) + jnp.where(two_in_a, parts[2], zero)
    in_b = jnp.where(one_in_a, zero, parts[1]) + jnp.where(two_in_a, zero, parts[2])
    readout = jnp.transpose(jnp.concatenate([in_a, in_b], axis=0))[:rows]
    await_pieces((0, 1))
    in_vecs = vectors(H * P_SIZE, (0, 1, 2))

    for gap in gaps:
        index = gap - X_LOW
        source = wrapped(me + gap, devices)
        when(
            needs_values(me, source),
            lambda: remote(
                piece, xs.at[index], x_send.at[index], x_recv.at[index], sq, me
            ).wait_recv(),
        )
    value_parts = []
    for r in range(2):
        part = jnp.zeros((half_rows, 128), F32)
        for gap in range(X_LOW, X_HIGH + 1):
            source = wrapped(me + gap, devices)
            start = value_offset(me, source)
            end = start + jnp.minimum(OWN_IN, H * P_SIZE - OWN_IN * source)
            wanted = needs_values(me, source)
            first = jnp.where(wanted, start, 128)
            by = lax.rem(start + 4 * H * P_SIZE - P_SIZE * r, 128)
            moved = pltpu.roll(xs[gap - X_LOW].astype(F32), by, 1)
            part = jnp.where((half_lane >= first) & (half_lane < end), moved, part)
        value_parts.append(part)
    values = jnp.concatenate(value_parts, axis=0)

    b16 = in_vecs.astype(BF16)
    scores = lax.dot_general(
        out_vecs.astype(BF16),
        jnp.concatenate([b16, b16], axis=0),
        (((1,), (1,)), ((), ())),
        preferred_element_type=F32,
    )
    cum_zero = jnp.where(has_zero_in_a, cum_a, cum_b)
    source_row = lane & (rows - 1)
    cum_across = jnp.sum(jnp.where(source_row == row, cum_zero, 0.0), axis=0, keepdims=True)
    before = ((source_row >> 3) == (row >> 3)) & (source_row <= row)
    mixing = jnp.where(before, jnp.exp(jnp.minimum(cum_zero - cum_across, 0.0)), 0.0) * scores
    high, low = split_two(mixing)
    v16 = values.astype(BF16)
    mixed = jnp.dot(
        jnp.where(lower, high, low).astype(BF16),
        jnp.concatenate([v16, v16], axis=0),
        preferred_element_type=F32,
    )
    zero_here = jnp.where(lower, 1, 0) == as_int(has_zero_in_a)
    drafts = jnp.where(zero_here, mixed * weight_zero, 0.0)

    features = readout + drafts
    held_end = P_SIZE * heads_of(me)

    def packed_for(gap):
        offset = OWN_OUT * wrapped(me + gap, devices) - P_SIZE * first_head
        offset = jnp.where(offset < -(H * P_SIZE) // 2, offset + H * P_SIZE, offset)
        offset = jnp.where(offset > (H * P_SIZE) // 2, offset - H * P_SIZE, offset)
        moved = pltpu.roll(features, lax.rem(4 * H * P_SIZE - offset, 128), 1)
        wanted = (lane < OWN_OUT) & (lane + offset >= 0) & (lane + offset < held_end)
        moved = jnp.where(wanted, moved, 0.0)
        return moved[:half_rows] + pltpu.roll(moved[half_rows:], P_SIZE, 1)

    for index, gap, _, _ in near:
        psend[index] = packed_for(gap)
    for index, gap, sends, _ in near:
        when(sends, lambda: partial_copy(index, gap).start())
    own = packed_for(0)

    turned = pltpu.roll(values, P_SIZE, 1)
    values_a = jnp.where(lower, values, turned) * decay_a
    values_b = jnp.where(lower, turned, values) * decay_b
    b3 = in_vecs.reshape(seqs, K, N)
    bb[...] = jnp.concatenate([b3, b3], axis=1).astype(BF16)
    for q in range(quads):
        level, in_a, real = of_lane(q)
        until = new_rows >> level
        inside = ((until & 1) == 1) & ((token_rows >> level) + 1 == until) & live & real
        term = jnp.where(inside, jnp.where(in_a, values_a, values_b), 0.0)
        high, low = split_two(term)
        both = jnp.concatenate(
            [high.reshape(seqs, K, 128), low.reshape(seqs, K, 128)], axis=1
        )
        xg[:, :, q * 128 : (q + 1) * 128] = both.astype(BF16)

    when(gets_low, lambda: low_copy().wait_recv())

    def update(s, carry):
        tokens = lax.dot_general(
            xg[s], bb[s], (((0,), (0,)), ((), ())), preferred_element_type=F32
        )
        came = jnp.where(gets_low, low_recv[s].astype(F32), 0.0)
        merged_a = low_a[s] + came
        merged_b = low_b[s]
        merged = (
            merged_a,
            jnp.where(split > block, merged_a, merged_b),
            jnp.where(split > 2 * block, merged_a, merged_b),
        )
        for j in range(LOCAL):
            at = slice(j * P_SIZE, (j + 1) * P_SIZE)
            new_ref[s, at, :] = (
                held[s, at, :] * stay_c[j, pl.ds(s, 1), :]
                + merged[j // block] * into_c[j, pl.ds(s, 1), :]
                + tokens[at, :]
            )
        return carry

    lax.fori_loop(0, seqs, update, 0)

    for index, gap, _, gets in near:
        when(
            gets,
            lambda: remote(
                psend.at[index], pslots.at[index], p_send.at[index], p_recv.at[index], sq, me
            ).wait_recv(),
        )
    total = own
    for index, _, _, gets in near:
        came = pslots[index]
        total = total + (came if gets is None else jnp.where(gets, came, 0.0))
    total = jnp.concatenate([total, pltpu.roll(total, P_SIZE, 1)], axis=0)
    out_ref[...] = total.reshape(seqs, K, 128)[:, :, 0:OWN_OUT].astype(BF16)

    @pl.when(me != 0)
    def _():
        remote(shared, shared, t_send.at[0], t_recv.at[0], sq, me).wait_recv()

    share_ref[...] = shared[0:1, 0:1] / (groups * seqs * K)

    @pl.when(is_source)
    def _():
        for r in range(columns - 1):
            y_copy(r).wait_send()

    @pl.when(has_slot)
    def _():
        for step in range(1, ROW):
            when(
                (y != columns - 1) | (lax.rem(z + step, ROW) != LATE),
                lambda: z_copy(step).wait_send(),
            )

    @pl.when(feeds_late)
    def _():
        for index in others:
            late_copy(index).wait_send()

    for gap in gaps:
        when(needs_values(wrapped(me - gap, devices), me), lambda: x_copy(gap).wait_send())
    when(sends_low, lambda: low_copy().wait_send())

    @pl.when(is_root)
    def _():
        for step in range(1, groups):
            count_copy(step).wait_send()
        for step in range(1, devices):
            total_copy(step).wait_send()

    for index, gap, sends, _ in near:
        when(sends, lambda: partial_copy(index, gap).wait_send())


def flush(new_in, out_in, new_out, out_out, sems):
    pieces = new_in.shape[0]
    copies = [pltpu.make_async_copy(out_in, out_out, sems.at[pieces])]
    copies += [pltpu.make_async_copy(new_in.at[s], new_out.at[s], sems.at[s]) for s in range(pieces)]
    for copy in copies:
        copy.start()
    for copy in copies:
        copy.wait()


def on_device(states, xbc, rates, level_weights, positions, accepted):
    devices = lax.axis_size("level")
    groups = lax.axis_size("seq")
    seqs = states.shape[0]
    rows = seqs * K
    wide = LOCAL * P_SIZE
    padded_wide = (LOCAL + 1) * P_SIZE
    vmem = pl.BlockSpec(memory_space=pltpu.VMEM)
    in_hbm = pl.BlockSpec(memory_space=pltpu.HBM)
    dma = pltpu.SemaphoreType.DMA
    x_slots = X_HIGH - X_LOW + 1
    outputs, new_states, share = pl.pallas_call(
        functools.partial(kernel, devices, groups),
        out_shape=(
            jax.ShapeDtypeStruct((seqs, K, OWN_OUT), BF16),
            jax.ShapeDtypeStruct((seqs, wide, N), F32),
            jax.ShapeDtypeStruct((1, 1), F32),
        ),
        in_specs=[in_hbm] * 6,
        out_specs=(vmem, vmem, vmem),
        scratch_shapes=[
            pltpu.VMEM(xbc.shape, BF16),
            pltpu.VMEM(rates.shape, F32),
            pltpu.VMEM(level_weights.shape, F32),
            pltpu.SMEM(positions.shape, jnp.int32),
            pltpu.SMEM(accepted.shape, jnp.int32),
            pltpu.VMEM((seqs, wide, N), F32),
            pltpu.VMEM((seqs, wide, 2 * N), BF16),
            pltpu.VMEM((rows, 128), F32),
            pltpu.VMEM((rows // 2, 128), BF16),
            pltpu.VMEM((BC_SLOTS, rows // 2, 128), BF16),
            pltpu.VMEM((x_slots, rows // 2, 128), BF16),
            pltpu.VMEM((seqs, P_SIZE, N), BF16),
            pltpu.VMEM((seqs, P_SIZE, N), BF16),
            pltpu.VMEM((seqs, P_SIZE, N), F32),
            pltpu.VMEM((seqs, P_SIZE, N), F32),
            pltpu.VMEM((LOCAL, seqs, 128), F32),
            pltpu.VMEM((LOCAL, seqs, 128), F32),
            pltpu.VMEM((LOCAL, seqs, 128), F32),
            pltpu.VMEM((seqs, LOCAL + 1, 128), F32),
            pltpu.VMEM((3, P_SIZE, 128), F32),
            pltpu.VMEM((2 * N, 128), BF16),
            pltpu.VMEM((seqs, 2 * K, N), BF16),
            pltpu.VMEM((seqs, 2 * K, padded_wide), BF16),
            pltpu.VMEM((3, rows // 2, 128), F32),
            pltpu.VMEM((3, rows // 2, 128), F32),
            pltpu.VMEM((groups, 8, 128), F32),
            pltpu.VMEM((8, 128), F32),
            dma((5,)),
            dma((seqs,)),
            dma((devices // ROW,)),
            dma((ROW,)),
            dma((x_slots,)),
            dma((BC_SLOTS,)),
            dma((x_slots,)),
            dma((2,)),
            dma((3,)),
            dma((3,)),
            dma((groups,)),
            dma((groups,)),
            dma((BC_SLOTS,)),
            dma((devices,)),
            dma((1,)),
        ],
        compiler_params=pltpu.CompilerParams(
            collective_id=0, has_side_effects=True, vmem_limit_bytes=40 << 20
        ),
    )(
        *[
            pltpu.with_memory_space_constraint(x, pltpu.HBM)
            for x in (
                states.reshape(seqs, wide, N),
                xbc,
                rates,
                level_weights,
                positions,
                accepted,
            )
        ]
    )
    anywhere = pl.BlockSpec(memory_space=pl.ANY)
    new_states, outputs = pl.pallas_call(
        flush,
        out_shape=(
            jax.ShapeDtypeStruct(new_states.shape, F32),
            jax.ShapeDtypeStruct(outputs.shape, BF16),
        ),
        in_specs=[anywhere, anywhere],
        out_specs=(in_hbm, in_hbm),
        scratch_shapes=[dma((seqs + 1,))],
        compiler_params=pltpu.CompilerParams(vmem_limit_bytes=4 << 20),
    )(new_states, outputs)
    return outputs, new_states.reshape(states.shape), share.reshape(())


def solution(mesh):
    in_specs = (
        P("seq", "level", None, None),
        P("seq", None, "level"),
        P("seq", None, None),
        P("seq", None, "level"),
        P("seq"),
        P("seq"),
    )
    out_specs = (P("seq", None, "level"), P("seq", "level", None, None), P())
    return jax.shard_map(
        on_device, mesh=mesh, in_specs=in_specs, out_specs=out_specs, check_vma=False
    )
```

```python
import functools

import jax
import jax.numpy as jnp
from jax import lax
from jax.experimental import pallas as pl
from jax.experimental.pallas import tpu as pltpu
from jax.sharding import PartitionSpec as P

H = 24
P_SIZE = 64
N = 128
L = 20
K = 8
ROW = 8
OWN_IN = 56
OWN_OUT = 48
LOCAL = 15
BC_FIRST = 27
BC_SLOTS = 5
LATE = 4
X_LOW, X_HIGH = -5, 2
MESH = pl.DeviceIdType.MESH
F32 = jnp.float32
BF16 = jnp.bfloat16


def first_head_of(d):
    return lax.rem(lax.div(LOCAL * d + L // 2, L), H)


def first_level_of(d):
    return lax.rem(LOCAL * d + L // 2, L)


def heads_of(d):
    return jnp.where(first_level_of(d) + LOCAL > L, 2, 1)


def value_offset(d, s):
    u = OWN_IN * s - P_SIZE * first_head_of(d)
    return jnp.where(u < -(H * P_SIZE) // 2, u + H * P_SIZE, u)


def needs_values(d, s):
    u = value_offset(d, s)
    return (s <= BC_FIRST) & (u > -OWN_IN) & (u < P_SIZE * heads_of(d))


def wrapped(d, devices):
    return lax.rem(d + devices, devices)


def as_int(x):
    return x.astype(jnp.int32)


def split_two(x):
    high = x.astype(BF16).astype(F32)
    return high, x - high


def kernel(
    devices,
    groups,
    states_ref,
    xbc_in,
    rates_in,
    weights_in,
    pos_in,
    acc_in,
    out_ref,
    new_ref,
    share_ref,
    xbc_ref,
    rates_ref,
    weights_ref,
    pos_ref,
    acc_ref,
    held,
    halves,
    padded,
    piece,
    bc,
    xs,
    low_send,
    low_recv,
    low_a,
    low_b,
    leave_c,
    stay_c,
    into_c,
    wide_w,
    parts,
    cc,
    bb,
    xg,
    psend,
    pslots,
    counts,
    shared,
    small_sem,
    in_sem,
    y_send,
    z_send,
    x_send,
    bc_recv,
    x_recv,
    low_sems,
    p_send,
    p_recv,
    n_send,
    n_recv,
    late_send,
    t_send,
    t_recv,
):
    seqs = xbc_ref.shape[0]
    rows = seqs * K
    me = lax.axis_index("level")
    sq = lax.axis_index("seq")
    y, z = lax.div(me, ROW), lax.rem(me, ROW)
    columns = devices // ROW
    first_z = BC_FIRST - (columns - 1) * ROW
    has_slot = z >= first_z
    is_source = has_slot & (y == columns - 1)
    is_late = (y == columns - 1) & (z == LATE)
    feeds_late = (y == 0) & (z == LATE)
    is_root = me == 0
    kind = lax.rem(me, 4)
    slot = jnp.maximum(z - first_z, 0)

    small = [
        pltpu.make_async_copy(src, dst, small_sem.at[i])
        for i, (src, dst) in enumerate(
            (
                (xbc_in, xbc_ref),
                (pos_in, pos_ref),
                (acc_in, acc_ref),
                (rates_in, rates_ref),
                (weights_in, weights_ref),
            )
        )
    ]

    def load(s):
        return pltpu.make_async_copy(states_ref.at[s], held.at[s], in_sem.at[s])

    for copy in small:
        copy.start()
    for s in range(seqs):
        load(s).start()

    barrier = pltpu.get_barrier_semaphore()

    def greet(group, level):
        pl.semaphore_signal(barrier, inc=1, device_id=(group, level), device_id_type=MESH)

    for other in range(first_z, ROW):

        @pl.when((z != other) & ((y != columns - 1) | (z != LATE) | (other == LATE)))
        def _():
            greet(sq, y * ROW + other)

    @pl.when(is_late)
    def _():
        greet(sq, LATE)

    @pl.when(has_slot & (y != columns - 1))
    def _():
        greet(sq, (columns - 1) * ROW + z)

    for gap in range(X_LOW, X_HIGH + 1):
        if gap != 0:
            source = wrapped(me + gap, devices)

            @pl.when(needs_values(me, source))
            def _():
                greet(sq, source)

    greet(sq, wrapped(me - 1, devices))

    @pl.when((kind == 1) | (kind == 2))
    def _():
        greet(sq, wrapped(me - 2, devices))

    @pl.when(kind == 2)
    def _():
        greet(sq, wrapped(me + 1, devices))

    @pl.when(is_root)
    def _():
        for step in range(1, groups):
            greet(lax.rem(sq + step, groups), me)

    @pl.when((z == 0) & (y != 0))
    def _():
        greet(sq, 0)

    @pl.when(z != 0)
    def _():
        greet(sq, y * ROW)

    expected = (ROW - 1) * as_int(has_slot) + (columns - 1) * as_int(is_source) + 1
    expected = expected - as_int(is_source & (z != LATE)) + as_int(feeds_late)
    expected = expected + (columns + groups - 2) * as_int(is_root)
    expected = expected + (ROW - 1) * as_int(z == 0)
    for gap in range(X_LOW, X_HIGH + 1):
        if gap != 0:
            expected = expected + as_int(needs_values(wrapped(me - gap, devices), me))
    expected = expected + as_int((kind == 0) | (kind == 3)) + as_int(kind == 3)

    lane = lax.broadcasted_iota(jnp.int32, (rows, 128), 1)
    lower = lane < P_SIZE
    half_rows = rows // 2
    half_lane = lane[:half_rows]
    half_lower = half_lane < P_SIZE

    padded[...] = jnp.zeros_like(padded)
    small[0].wait()
    padded[:, 0:OWN_IN] = xbc_ref[...].astype(F32).reshape(rows, OWN_IN)
    wide = padded[...]
    packed = jnp.where(half_lower, wide[:half_rows], pltpu.roll(wide[half_rows:], P_SIZE, 1))
    packed = packed.astype(BF16)
    piece[...] = packed
    xs[-X_LOW] = packed

    @pl.when(is_source)
    def _():
        bc[slot] = packed

    small[1].wait()
    small[2].wait()
    sub = lax.broadcasted_iota(jnp.int32, (seqs, 128), 0)
    pos_s = jnp.zeros((seqs, 128), jnp.int32)
    acc_s = jnp.zeros((seqs, 128), jnp.int32)
    for s in range(seqs):
        pos_s = jnp.where(sub == s, pos_ref[s], pos_s)
        acc_s = jnp.where(sub == s, acc_ref[s], acc_s)
    new_s = pos_s + acc_s
    changed = pos_s ^ new_s
    level_0 = first_level_of(me)
    split = jnp.minimum(L - level_0, LOCAL)
    levels = [lax.rem(level_0 + j, L) for j in range(LOCAL)] + [0]
    block = LOCAL // 3
    one_in_a, two_in_a = split > block, split > 2 * block
    has_zero_in_a = level_0 == 0

    for j in range(LOCAL):
        occupied = (pos_s >> levels[j]) & 1
        above = changed >> levels[j]
        leave_c[j] = jnp.where((above >> 1) != 0, occupied, 0).astype(F32)

    def gather_low(s, carry):
        load(s).wait()
        sums = []
        for part in range(3):
            total = None
            for j in range(part * block, (part + 1) * block):
                x = held[s, j * P_SIZE : (j + 1) * P_SIZE, :]
                high, low = split_two(x)
                halves[s, j * P_SIZE : (j + 1) * P_SIZE, 0:N] = high.astype(BF16)
                halves[s, j * P_SIZE : (j + 1) * P_SIZE, N : 2 * N] = low.astype(BF16)
                term = x * leave_c[j, pl.ds(s, 1), :]
                total = term if total is None else total + term
            sums.append(total)
        zero = jnp.zeros_like(sums[0])
        in_a = sums[0] + jnp.where(one_in_a, sums[1], zero) + jnp.where(two_in_a, sums[2], zero)
        in_b = jnp.where(one_in_a, zero, sums[1]) + jnp.where(two_in_a, zero, sums[2])
        low_a[s] = in_a
        low_b[s] = in_b
        low_send[s] = jnp.where(has_zero_in_a, in_a, in_b).astype(BF16)
        return carry

    @pl.when(z < first_z)
    def _():
        lax.fori_loop(0, seqs, gather_low, 0)

    @pl.when(is_root)
    def _():
        taken_here = jnp.int32(0)
        for s in range(seqs):
            taken_here = taken_here + acc_ref[s]
        counts[sq] = jnp.full((8, 128), taken_here, jnp.int32).astype(F32)

    pl.semaphore_wait(barrier, expected)

    def remote(src, dst, send_sem, recv_sem, group, level):
        return pltpu.make_async_remote_copy(
            src_ref=src,
            dst_ref=dst,
            send_sem=send_sem,
            recv_sem=recv_sem,
            device_id=(group, level),
            device_id_type=MESH,
        )

    def y_copy(row):
        return remote(bc.at[slot], bc.at[slot], y_send.at[row], bc_recv.at[slot], sq, row * ROW + z)

    def z_copy(step):
        other = y * ROW + lax.rem(z + step, ROW)
        return remote(bc.at[slot], bc.at[slot], z_send.at[step], bc_recv.at[slot], sq, other)

    def x_copy(gap):
        target = wrapped(me - gap, devices)
        index = gap - X_LOW
        return remote(piece, xs.at[index], x_send.at[index], x_recv.at[index], sq, target)

    def low_copy():
        target = wrapped(me + 1, devices)
        return remote(low_send, low_recv, low_sems.at[0], low_sems.at[1], sq, target)

    def count_copy(step):
        return remote(
            counts.at[sq], counts.at[sq], n_send.at[step], n_recv.at[sq], lax.rem(sq + step, groups), me
        )

    others = [index for index in range(BC_SLOTS) if index != LATE - first_z]

    def late_copy(index):
        target = (columns - 1) * ROW + LATE
        return remote(bc.at[index], bc.at[index], late_send.at[index], bc_recv.at[index], sq, target)

    def column_copy(r):
        return remote(shared, shared, t_send.at[ROW + r], t_recv.at[0], sq, r * ROW)

    def row_copy(step):
        return remote(shared, shared, t_send.at[step], t_recv.at[0], sq, y * ROW + step)

    def await_total():
        remote(shared, shared, t_send.at[0], t_recv.at[0], sq, me).wait_recv()

    def partial_copy(index, gap):
        target = wrapped(me + gap, devices)
        return remote(psend.at[index], pslots.at[index], p_send.at[index], p_recv.at[index], sq, target)

    sends_low = kind != 1
    gets_low = kind != 2
    gaps = [gap for gap in range(X_LOW, X_HIGH + 1) if gap != 0]
    near = (
        (0, 2, (kind == 0) | (kind == 3), (kind == 1) | (kind == 2)),
        (1, 1, None, None),
        (2, -1, kind == 3, kind == 2),
    )

    def when(cond, do):
        if cond is None:
            do()
        else:
            pl.when(cond)(do)

    z_steps = (4, 3, 5, 2, 6, 1, 7)

    @pl.when(is_source)
    def _():
        for r in range(columns - 1):
            y_copy(r).start()
        for step in z_steps:
            when(lax.rem(z + step, ROW) != LATE, lambda: z_copy(step).start())

    for gap in gaps:
        when(needs_values(wrapped(me - gap, devices), me), lambda: x_copy(gap).start())
    @pl.when(is_root)
    def _():
        for step in range(1, groups):
            count_copy(step).start()


    @pl.when(has_slot)
    def _():
        lax.fori_loop(0, seqs, gather_low, 0)

    when(sends_low, lambda: low_copy().start())

    @pl.when(has_slot & (y != columns - 1))
    def _():
        remote(bc.at[slot], bc.at[slot], y_send.at[0], bc_recv.at[slot], sq, me).wait_recv()
        for step in z_steps:
            z_copy(step).start()

    head_lane = lax.broadcasted_iota(jnp.int32, (rows, H), 1)
    small[3].wait()
    small[4].wait()
    rates = rates_ref[...].reshape(rows, H)
    first_head = first_head_of(me)
    second_head = lax.rem(first_head + 1, H)
    row = lax.broadcasted_iota(jnp.int32, (rows, 128), 0)
    token = row & (K - 1)
    pos_rows = jnp.concatenate([jnp.full((K, 128), pos_ref[s], jnp.int32) for s in range(seqs)], 0)
    acc_rows = jnp.concatenate([jnp.full((K, 128), acc_ref[s], jnp.int32) for s in range(seqs)], 0)
    new_rows = pos_rows + acc_rows
    token_rows = pos_rows + token
    live = token < acc_rows

    def decays(head):
        rate = jnp.sum(jnp.where(head_lane == head, rates, 0.0), axis=1, keepdims=True)
        rate = jnp.broadcast_to(rate, (rows, 128))
        running = rate
        for by in (1, 2, 4):
            running = running + jnp.where(token >= by, pltpu.roll(running, by, 0), 0.0)
        cum = -running
        taken = -jnp.sum(jnp.where(live, rate, 0.0).reshape(seqs, K, 128), axis=1)
        taken_rows = jnp.broadcast_to(taken[:, None, :], (seqs, K, 128)).reshape(rows, 128)
        decay = jnp.where(live, jnp.exp(jnp.minimum(taken_rows - cum, 0.0)), 0.0)
        return cum, jnp.exp(cum), jnp.exp(taken), decay

    cum_a, grown_a, kept_a, decay_a = decays(first_head)
    cum_b, grown_b, kept_b, decay_b = decays(second_head)

    for j in range(LOCAL):
        in_a = j < split
        kept = jnp.where(in_a, kept_a, kept_b)
        occupied = (pos_s >> levels[j]) & 1
        new_occupied = (new_s >> levels[j]) & 1
        above = changed >> levels[j]
        stay_c[j] = jnp.where((above == 0) & (occupied == 1) & (new_occupied == 1), kept, 0.0)
        into_c[j] = jnp.where((above == 1) & (new_occupied == 1), kept, 0.0)

    weights = weights_ref[...].reshape(rows, LOCAL)
    local_lane = lax.broadcasted_iota(jnp.int32, (rows, LOCAL), 1)
    level_lane = lax.rem(level_0 + local_lane, L)
    weight_zero = jnp.sum(jnp.where(level_lane == 0, weights, 0.0), axis=1, keepdims=True)
    quads = (LOCAL + 1) // 2

    def of_lane(q):
        two = 2 * q + jnp.where(lower, 0, 1)
        return jnp.where(lower, levels[2 * q], levels[2 * q + 1]), two < split, two < LOCAL

    padded[:, 0:LOCAL] = weights
    here = lane < LOCAL
    level = level_0 + jnp.where(here, lane, 0)
    level = jnp.where(level >= L, level - L, level)
    shown = here & (((pos_rows >> level) & 1) == 1)
    by_token = jnp.where(shown, padded[...] * jnp.where(lane < split, grown_a, grown_b), 0.0)
    by_level = jnp.transpose(jnp.concatenate([by_token, jnp.zeros_like(by_token)], axis=0))
    by_level = by_level[: LOCAL + 1]
    for s in range(seqs):
        wide_w[s] = jnp.where((lane[: LOCAL + 1] >> 3) == s, by_level, 0.0)
    parts[...] = jnp.zeros_like(parts)

    for gap in gaps:
        index = gap - X_LOW
        source = wrapped(me + gap, devices)
        when(
            needs_values(me, source),
            lambda: remote(
                piece, xs.at[index], x_send.at[index], x_recv.at[index], sq, me
            ).wait_recv(),
        )
    value_parts = []
    for r in range(2):
        part = jnp.zeros((half_rows, 128), F32)
        for gap in range(X_LOW, X_HIGH + 1):
            source = wrapped(me + gap, devices)
            start = value_offset(me, source)
            end = start + jnp.minimum(OWN_IN, H * P_SIZE - OWN_IN * source)
            wanted = needs_values(me, source)
            first = jnp.where(wanted, start, 128)
            by = lax.rem(start + 4 * H * P_SIZE - P_SIZE * r, 128)
            moved = pltpu.roll(xs[gap - X_LOW].astype(F32), by, 1)
            part = jnp.where((half_lane >= first) & (half_lane < end), moved, part)
        value_parts.append(part)
    values = jnp.concatenate(value_parts, axis=0)

    turned = pltpu.roll(values, P_SIZE, 1)
    values_a = jnp.where(lower, values, turned) * decay_a
    values_b = jnp.where(lower, turned, values) * decay_b
    for q in range(quads):
        level, in_a, real = of_lane(q)
        until = new_rows >> level
        inside = ((until & 1) == 1) & ((token_rows >> level) + 1 == until) & live & real
        term = jnp.where(inside, jnp.where(in_a, values_a, values_b), 0.0)
        high, low = split_two(term)
        both = jnp.concatenate(
            [high.reshape(seqs, K, 128), low.reshape(seqs, K, 128)], axis=1
        )
        xg[:, :, q * 128 : (q + 1) * 128] = both.astype(BF16)

    @pl.when(is_root)
    def _():
        for step in range(1, groups):
            other = lax.rem(sq + step, groups)
            remote(
                counts.at[other], counts.at[other], n_send.at[step], n_recv.at[other], sq, me
            ).wait_recv()
        shared[...] = jnp.sum(counts[...], axis=0)
        for r in range(1, columns):
            column_copy(r).start()

    @pl.when(z == 0)
    def _():
        pl.when(y != 0)(await_total)
        for step in range(1, ROW):
            row_copy(step).start()

    def await_pieces(indices):
        for index in indices:

            @pl.when(z != first_z + index)
            def _():
                remote(
                    bc.at[index], bc.at[index], y_send.at[0], bc_recv.at[index], sq, me
                ).wait_recv()

        for index in indices:
            if index in others:

                @pl.when(feeds_late)
                def _():
                    late_copy(index).start()

    def vectors(first_feature, indices):
        pair = []
        got = [bc[i].astype(F32) for i in indices]
        for r in range(2):
            part = jnp.zeros((half_rows, 128), F32)
            for i, moved in zip(indices, got):
                start = OWN_IN * (BC_FIRST + i) - first_feature
                by = (start - P_SIZE * r) % 128
                if by:
                    moved = pltpu.roll(moved, by, 1)
                part = jnp.where((half_lane >= start) & (half_lane < start + OWN_IN), moved, part)
            pair.append(part)
        return jnp.concatenate(pair, axis=0)

    await_pieces((2, 3, 4))
    out_vecs = vectors(H * P_SIZE + N, (2, 3, 4))
    across = jnp.transpose(jnp.concatenate([out_vecs, jnp.zeros_like(out_vecs)], axis=0))
    across = across.astype(BF16)
    cc[0:N, :] = across
    cc[N : 2 * N, :] = across

    def read_out(s, carry):
        size = block * P_SIZE
        for part in range(3):
            read = jnp.dot(
                halves[s, part * size : (part + 1) * size, :], cc[...], preferred_element_type=F32
            )
            total = parts[part]
            for i in range(block):
                j = part * block + i
                total = total + read[i * P_SIZE : (i + 1) * P_SIZE, :] * wide_w[s, j : j + 1, :]
            parts[part] = total
        return carry

    lax.fori_loop(0, seqs, read_out, 0, unroll=2)

    zero = jnp.zeros((P_SIZE, 128), F32)
    in_a = parts[0] + jnp.where(one_in_a, parts[1], zero) + jnp.where(two_in_a, parts[2], zero)
    in_b = jnp.where(one_in_a, zero, parts[1]) + jnp.where(two_in_a, zero, parts[2])
    readout = jnp.transpose(jnp.concatenate([in_a, in_b], axis=0))[:rows]
    await_pieces((0, 1))
    in_vecs = vectors(H * P_SIZE, (0, 1, 2))

    b16 = in_vecs.astype(BF16)
    scores = lax.dot_general(
        out_vecs.astype(BF16),
        jnp.concatenate([b16, b16], axis=0),
        (((1,), (1,)), ((), ())),
        preferred_element_type=F32,
    )
    cum_zero = jnp.where(has_zero_in_a, cum_a, cum_b)
    source_row = lane & (rows - 1)
    cum_across = jnp.sum(jnp.where(source_row == row, cum_zero, 0.0), axis=0, keepdims=True)
    before = ((source_row >> 3) == (row >> 3)) & (source_row <= row)
    mixing = jnp.where(before, jnp.exp(jnp.minimum(cum_zero - cum_across, 0.0)), 0.0) * scores
    high, low = split_two(mixing)
    v16 = values.astype(BF16)
    mixed = jnp.dot(
        jnp.where(lower, high, low).astype(BF16),
        jnp.concatenate([v16, v16], axis=0),
        preferred_element_type=F32,
    )
    zero_here = jnp.where(lower, 1, 0) == as_int(has_zero_in_a)
    drafts = jnp.where(zero_here, mixed * weight_zero, 0.0)

    features = readout + drafts
    held_end = P_SIZE * heads_of(me)

    def packed_for(gap):
        offset = OWN_OUT * wrapped(me + gap, devices) - P_SIZE * first_head
        offset = jnp.where(offset < -(H * P_SIZE) // 2, offset + H * P_SIZE, offset)
        offset = jnp.where(offset > (H * P_SIZE) // 2, offset - H * P_SIZE, offset)
        moved = pltpu.roll(features, lax.rem(4 * H * P_SIZE - offset, 128), 1)
        wanted = (lane < OWN_OUT) & (lane + offset >= 0) & (lane + offset < held_end)
        moved = jnp.where(wanted, moved, 0.0)
        return moved[:half_rows] + pltpu.roll(moved[half_rows:], P_SIZE, 1)

    for index, gap, sends, _ in near:
        psend[index] = packed_for(gap)
        when(sends, lambda: partial_copy(index, gap).start())
    own = packed_for(0)

    b3 = in_vecs.reshape(seqs, K, N)
    bb[...] = jnp.concatenate([b3, b3], axis=1).astype(BF16)
    when(gets_low, lambda: low_copy().wait_recv())

    def update(s, carry):
        tokens = lax.dot_general(
            xg[s], bb[s], (((0,), (0,)), ((), ())), preferred_element_type=F32
        )
        came = jnp.where(gets_low, low_recv[s].astype(F32), 0.0)
        merged_a = low_a[s] + came
        merged_b = low_b[s]
        merged = (
            merged_a,
            jnp.where(split > block, merged_a, merged_b),
            jnp.where(split > 2 * block, merged_a, merged_b),
        )
        for j in range(LOCAL):
            at = slice(j * P_SIZE, (j + 1) * P_SIZE)
            new_ref[s, at, :] = (
                held[s, at, :] * stay_c[j, pl.ds(s, 1), :]
                + merged[j // block] * into_c[j, pl.ds(s, 1), :]
                + tokens[at, :]
            )
        return carry

    lax.fori_loop(0, seqs, update, 0)

    for index, gap, _, gets in near:
        when(
            gets,
            lambda: remote(
                psend.at[index], pslots.at[index], p_send.at[index], p_recv.at[index], sq, me
            ).wait_recv(),
        )
    total = own
    for index, _, _, gets in near:
        came = pslots[index]
        total = total + (came if gets is None else jnp.where(gets, came, 0.0))
    total = jnp.concatenate([total, pltpu.roll(total, P_SIZE, 1)], axis=0)
    out_ref[...] = total.reshape(seqs, K, 128)[:, :, 0:OWN_OUT].astype(BF16)

    pl.when(z != 0)(await_total)
    share_ref[...] = shared[0:1, 0:1] / (groups * seqs * K)

    @pl.when(is_source)
    def _():
        for r in range(columns - 1):
            y_copy(r).wait_send()

    @pl.when(has_slot)
    def _():
        for step in range(1, ROW):
            when(
                (y != columns - 1) | (lax.rem(z + step, ROW) != LATE),
                lambda: z_copy(step).wait_send(),
            )

    @pl.when(feeds_late)
    def _():
        for index in others:
            late_copy(index).wait_send()

    for gap in gaps:
        when(needs_values(wrapped(me - gap, devices), me), lambda: x_copy(gap).wait_send())
    when(sends_low, lambda: low_copy().wait_send())

    @pl.when(is_root)
    def _():
        for step in range(1, groups):
            count_copy(step).wait_send()
        for r in range(1, columns):
            column_copy(r).wait_send()

    @pl.when(z == 0)
    def _():
        for step in range(1, ROW):
            row_copy(step).wait_send()

    for index, gap, sends, _ in near:
        when(sends, lambda: partial_copy(index, gap).wait_send())


def flush(new_in, out_in, new_out, out_out, sems):
    pieces = new_in.shape[0]
    copies = [pltpu.make_async_copy(out_in, out_out, sems.at[pieces])]
    copies += [pltpu.make_async_copy(new_in.at[s], new_out.at[s], sems.at[s]) for s in range(pieces)]
    for copy in copies:
        copy.start()
    for copy in copies:
        copy.wait()


def on_device(states, xbc, rates, level_weights, positions, accepted):
    devices = lax.axis_size("level")
    groups = lax.axis_size("seq")
    seqs = states.shape[0]
    rows = seqs * K
    wide = LOCAL * P_SIZE
    padded_wide = (LOCAL + 1) * P_SIZE
    vmem = pl.BlockSpec(memory_space=pltpu.VMEM)
    in_hbm = pl.BlockSpec(memory_space=pltpu.HBM)
    dma = pltpu.SemaphoreType.DMA
    x_slots = X_HIGH - X_LOW + 1
    outputs, new_states, share = pl.pallas_call(
        functools.partial(kernel, devices, groups),
        out_shape=(
            jax.ShapeDtypeStruct((seqs, K, OWN_OUT), BF16),
            jax.ShapeDtypeStruct((seqs, wide, N), F32),
            jax.ShapeDtypeStruct((1, 1), F32),
        ),
        in_specs=[in_hbm] * 6,
        out_specs=(vmem, vmem, vmem),
        scratch_shapes=[
            pltpu.VMEM(xbc.shape, BF16),
            pltpu.VMEM(rates.shape, F32),
            pltpu.VMEM(level_weights.shape, F32),
            pltpu.SMEM(positions.shape, jnp.int32),
            pltpu.SMEM(accepted.shape, jnp.int32),
            pltpu.VMEM((seqs, wide, N), F32),
            pltpu.VMEM((seqs, wide, 2 * N), BF16),
            pltpu.VMEM((rows, 128), F32),
            pltpu.VMEM((rows // 2, 128), BF16),
            pltpu.VMEM((BC_SLOTS, rows // 2, 128), BF16),
            pltpu.VMEM((x_slots, rows // 2, 128), BF16),
            pltpu.VMEM((seqs, P_SIZE, N), BF16),
            pltpu.VMEM((seqs, P_SIZE, N), BF16),
            pltpu.VMEM((seqs, P_SIZE, N), F32),
            pltpu.VMEM((seqs, P_SIZE, N), F32),
            pltpu.VMEM((LOCAL, seqs, 128), F32),
            pltpu.VMEM((LOCAL, seqs, 128), F32),
            pltpu.VMEM((LOCAL, seqs, 128), F32),
            pltpu.VMEM((seqs, LOCAL + 1, 128), F32),
            pltpu.VMEM((3, P_SIZE, 128), F32),
            pltpu.VMEM((2 * N, 128), BF16),
            pltpu.VMEM((seqs, 2 * K, N), BF16),
            pltpu.VMEM((seqs, 2 * K, padded_wide), BF16),
            pltpu.VMEM((3, rows // 2, 128), F32),
            pltpu.VMEM((3, rows // 2, 128), F32),
            pltpu.VMEM((groups, 8, 128), F32),
            pltpu.VMEM((8, 128), F32),
            dma((5,)),
            dma((seqs,)),
            dma((devices // ROW,)),
            dma((ROW,)),
            dma((x_slots,)),
            dma((BC_SLOTS,)),
            dma((x_slots,)),
            dma((2,)),
            dma((3,)),
            dma((3,)),
            dma((groups,)),
            dma((groups,)),
            dma((BC_SLOTS,)),
            dma((ROW + devices // ROW,)),
            dma((1,)),
        ],
        compiler_params=pltpu.CompilerParams(
            collective_id=0, has_side_effects=True, vmem_limit_bytes=40 << 20
        ),
    )(
        *[
            pltpu.with_memory_space_constraint(x, pltpu.HBM)
            for x in (
                states.reshape(seqs, wide, N),
                xbc,
                rates,
                level_weights,
                positions,
                accepted,
            )
        ]
    )
    anywhere = pl.BlockSpec(memory_space=pl.ANY)
    new_states, outputs = pl.pallas_call(
        flush,
        out_shape=(
            jax.ShapeDtypeStruct(new_states.shape, F32),
            jax.ShapeDtypeStruct(outputs.shape, BF16),
        ),
        in_specs=[anywhere, anywhere],
        out_specs=(in_hbm, in_hbm),
        scratch_shapes=[dma((seqs + 1,))],
        compiler_params=pltpu.CompilerParams(vmem_limit_bytes=4 << 20),
    )(new_states, outputs)
    return outputs, new_states.reshape(states.shape), share.reshape(())


def solution(mesh):
    in_specs = (
        P("seq", "level", None, None),
        P("seq", None, "level"),
        P("seq", None, None),
        P("seq", None, "level"),
        P("seq"),
        P("seq"),
    )
    out_specs = (P("seq", None, "level"), P("seq", "level", None, None), P())
    return jax.shard_map(
        on_device, mesh=mesh, in_specs=in_specs, out_specs=out_specs, check_vma=False
    )
```

```python
import functools

import jax
import jax.numpy as jnp
from jax import lax
from jax.experimental import pallas as pl
from jax.experimental.pallas import tpu as pltpu
from jax.sharding import PartitionSpec as P

H = 24
P_SIZE = 64
N = 128
L = 20
K = 8
ROW = 8
OWN_IN = 56
OWN_OUT = 48
LOCAL = 15
BC_FIRST = 27
BC_SLOTS = 5
LATE = 4
X_LOW, X_HIGH = -5, 2
MESH = pl.DeviceIdType.MESH
F32 = jnp.float32
BF16 = jnp.bfloat16


def first_head_of(d):
    return lax.rem(lax.div(LOCAL * d + L // 2, L), H)


def first_level_of(d):
    return lax.rem(LOCAL * d + L // 2, L)


def heads_of(d):
    return jnp.where(first_level_of(d) + LOCAL > L, 2, 1)


def value_offset(d, s):
    u = OWN_IN * s - P_SIZE * first_head_of(d)
    return jnp.where(u < -(H * P_SIZE) // 2, u + H * P_SIZE, u)


def needs_values(d, s):
    u = value_offset(d, s)
    return (s <= BC_FIRST) & (u > -OWN_IN) & (u < P_SIZE * heads_of(d))


def wrapped(d, devices):
    return lax.rem(d + devices, devices)


def as_int(x):
    return x.astype(jnp.int32)


def split_two(x):
    high = x.astype(BF16).astype(F32)
    return high, x - high


def kernel(
    devices,
    groups,
    states_ref,
    xbc_in,
    rates_in,
    weights_in,
    pos_in,
    acc_in,
    out_ref,
    new_ref,
    share_ref,
    xbc_ref,
    rates_ref,
    weights_ref,
    pos_ref,
    acc_ref,
    held,
    halves,
    padded,
    piece,
    bc,
    xs,
    low_send,
    low_recv,
    low_a,
    low_b,
    leave_c,
    stay_c,
    into_c,
    wide_w,
    parts,
    cc,
    bb,
    xg,
    psend,
    pslots,
    counts,
    shared,
    small_sem,
    in_sem,
    y_send,
    z_send,
    x_send,
    bc_recv,
    x_recv,
    low_sems,
    p_send,
    p_recv,
    n_send,
    n_recv,
    late_send,
    t_send,
    t_recv,
):
    seqs = xbc_ref.shape[0]
    rows = seqs * K
    me = lax.axis_index("level")
    sq = lax.axis_index("seq")
    y, z = lax.div(me, ROW), lax.rem(me, ROW)
    columns = devices // ROW
    first_z = BC_FIRST - (columns - 1) * ROW
    has_slot = z >= first_z
    is_source = has_slot & (y == columns - 1)
    is_late = (y == columns - 1) & (z == LATE)
    feeds_late = (y == 0) & (z == LATE)
    is_root = me == 0
    kind = lax.rem(me, 4)
    slot = jnp.maximum(z - first_z, 0)

    small = [
        pltpu.make_async_copy(src, dst, small_sem.at[i])
        for i, (src, dst) in enumerate(
            (
                (xbc_in, xbc_ref),
                (pos_in, pos_ref),
                (acc_in, acc_ref),
                (rates_in, rates_ref),
                (weights_in, weights_ref),
            )
        )
    ]

    def load(s):
        return pltpu.make_async_copy(states_ref.at[s], held.at[s], in_sem.at[s])

    for copy in small:
        copy.start()
    for s in range(seqs):
        load(s).start()

    barrier = pltpu.get_barrier_semaphore()

    def greet(group, level):
        pl.semaphore_signal(barrier, inc=1, device_id=(group, level), device_id_type=MESH)

    for other in range(first_z, ROW):

        @pl.when((z != other) & ((y != columns - 1) | (z != LATE) | (other == LATE)))
        def _():
            greet(sq, y * ROW + other)

    @pl.when(is_late)
    def _():
        greet(sq, LATE)

    @pl.when(has_slot & (y != columns - 1))
    def _():
        greet(sq, (columns - 1) * ROW + z)

    for gap in range(X_LOW, X_HIGH + 1):
        if gap != 0:
            source = wrapped(me + gap, devices)

            @pl.when(needs_values(me, source))
            def _():
                greet(sq, source)

    greet(sq, wrapped(me - 1, devices))

    @pl.when((kind == 1) | (kind == 2))
    def _():
        greet(sq, wrapped(me - 2, devices))

    @pl.when(kind == 2)
    def _():
        greet(sq, wrapped(me + 1, devices))

    @pl.when(is_root)
    def _():
        for step in range(1, groups):
            greet(lax.rem(sq + step, groups), me)

    @pl.when(me != 0)
    def _():
        greet(sq, 0)

    expected = (ROW - 1) * as_int(has_slot) + (columns - 1) * as_int(is_source) + 1
    expected = expected - as_int(is_source & (z != LATE)) + as_int(feeds_late)
    expected = expected + (devices + groups - 2) * as_int(is_root)
    for gap in range(X_LOW, X_HIGH + 1):
        if gap != 0:
            expected = expected + as_int(needs_values(wrapped(me - gap, devices), me))
    expected = expected + as_int((kind == 0) | (kind == 3)) + as_int(kind == 3)

    lane = lax.broadcasted_iota(jnp.int32, (rows, 128), 1)
    lower = lane < P_SIZE
    half_rows = rows // 2
    half_lane = lane[:half_rows]
    half_lower = half_lane < P_SIZE

    padded[...] = jnp.zeros_like(padded)
    small[0].wait()
    padded[:, 0:OWN_IN] = xbc_ref[...].astype(F32).reshape(rows, OWN_IN)
    wide = padded[...]
    packed = jnp.where(half_lower, wide[:half_rows], pltpu.roll(wide[half_rows:], P_SIZE, 1))
    packed = packed.astype(BF16)
    piece[...] = packed
    xs[-X_LOW] = packed

    @pl.when(is_source)
    def _():
        bc[slot] = packed

    small[1].wait()
    small[2].wait()
    sub = lax.broadcasted_iota(jnp.int32, (seqs, 128), 0)
    pos_s = jnp.zeros((seqs, 128), jnp.int32)
    acc_s = jnp.zeros((seqs, 128), jnp.int32)
    for s in range(seqs):
        pos_s = jnp.where(sub == s, pos_ref[s], pos_s)
        acc_s = jnp.where(sub == s, acc_ref[s], acc_s)
    new_s = pos_s + acc_s
    changed = pos_s ^ new_s
    level_0 = first_level_of(me)
    split = jnp.minimum(L - level_0, LOCAL)
    levels = [lax.rem(level_0 + j, L) for j in range(LOCAL)] + [0]
    block = LOCAL // 3
    one_in_a, two_in_a = split > block, split > 2 * block
    has_zero_in_a = level_0 == 0

    for j in range(LOCAL):
        occupied = (pos_s >> levels[j]) & 1
        above = changed >> levels[j]
        leave_c[j] = jnp.where((above >> 1) != 0, occupied, 0).astype(F32)

    def gather_low(s, carry):
        load(s).wait()
        sums = []
        for part in range(3):
            total = None
            for j in range(part * block, (part + 1) * block):
                x = held[s, j * P_SIZE : (j + 1) * P_SIZE, :]
                high, low = split_two(x)
                halves[s, j * P_SIZE : (j + 1) * P_SIZE, 0:N] = high.astype(BF16)
                halves[s, j * P_SIZE : (j + 1) * P_SIZE, N : 2 * N] = low.astype(BF16)
                term = x * leave_c[j, pl.ds(s, 1), :]
                total = term if total is None else total + term
            sums.append(total)
        zero = jnp.zeros_like(sums[0])
        in_a = sums[0] + jnp.where(one_in_a, sums[1], zero) + jnp.where(two_in_a, sums[2], zero)
        in_b = jnp.where(one_in_a, zero, sums[1]) + jnp.where(two_in_a, zero, sums[2])
        low_a[s] = in_a
        low_b[s] = in_b
        low_send[s] = jnp.where(has_zero_in_a, in_a, in_b).astype(BF16)
        return carry

    @pl.when(jnp.logical_not(is_source))
    def _():
        lax.fori_loop(0, seqs, gather_low, 0)

    @pl.when(is_root)
    def _():
        taken_here = jnp.int32(0)
        for s in range(seqs):
            taken_here = taken_here + acc_ref[s]
        counts[sq] = jnp.full((8, 128), taken_here, jnp.int32).astype(F32)

    pl.semaphore_wait(barrier, expected)

    def remote(src, dst, send_sem, recv_sem, group, level):
        return pltpu.make_async_remote_copy(
            src_ref=src,
            dst_ref=dst,
            send_sem=send_sem,
            recv_sem=recv_sem,
            device_id=(group, level),
            device_id_type=MESH,
        )

    def y_copy(row):
        return remote(bc.at[slot], bc.at[slot], y_send.at[row], bc_recv.at[slot], sq, row * ROW + z)

    def z_copy(step):
        other = y * ROW + lax.rem(z + step, ROW)
        return remote(bc.at[slot], bc.at[slot], z_send.at[step], bc_recv.at[slot], sq, other)

    def x_copy(gap):
        target = wrapped(me - gap, devices)
        index = gap - X_LOW
        return remote(piece, xs.at[index], x_send.at[index], x_recv.at[index], sq, target)

    def low_copy():
        target = wrapped(me + 1, devices)
        return remote(low_send, low_recv, low_sems.at[0], low_sems.at[1], sq, target)

    def count_copy(step):
        return remote(
            counts.at[sq], counts.at[sq], n_send.at[step], n_recv.at[sq], lax.rem(sq + step, groups), me
        )

    others = [index for index in range(BC_SLOTS) if index != LATE - first_z]

    def late_copy(index):
        target = (columns - 1) * ROW + LATE
        return remote(bc.at[index], bc.at[index], late_send.at[index], bc_recv.at[index], sq, target)

    def total_copy(step):
        return remote(shared, shared, t_send.at[step], t_recv.at[0], sq, step)

    def partial_copy(index, gap):
        target = wrapped(me + gap, devices)
        return remote(psend.at[index], pslots.at[index], p_send.at[index], p_recv.at[index], sq, target)

    sends_low = kind != 1
    gets_low = kind != 2
    gaps = [gap for gap in range(X_LOW, X_HIGH + 1) if gap != 0]
    near = (
        (0, 2, (kind == 0) | (kind == 3), (kind == 1) | (kind == 2)),
        (1, 1, None, None),
        (2, -1, kind == 3, kind == 2),
    )

    def when(cond, do):
        if cond is None:
            do()
        else:
            pl.when(cond)(do)

    z_steps = (4, 3, 5, 2, 6, 1, 7)

    @pl.when(is_source)
    def _():
        for r in range(columns - 1):
            y_copy(r).start()
        for step in z_steps:
            when(lax.rem(z + step, ROW) != LATE, lambda: z_copy(step).start())

    for gap in gaps:
        when(needs_values(wrapped(me - gap, devices), me), lambda: x_copy(gap).start())
    @pl.when(is_root)
    def _():
        for step in range(1, groups):
            count_copy(step).start()


    @pl.when(is_source)
    def _():
        lax.fori_loop(0, seqs, gather_low, 0)

    when(sends_low, lambda: low_copy().start())

    @pl.when(has_slot & (y != columns - 1))
    def _():
        remote(bc.at[slot], bc.at[slot], y_send.at[0], bc_recv.at[slot], sq, me).wait_recv()
        for step in z_steps:
            z_copy(step).start()

    head_lane = lax.broadcasted_iota(jnp.int32, (rows, H), 1)
    small[3].wait()
    small[4].wait()
    rates = rates_ref[...].reshape(rows, H)
    first_head = first_head_of(me)
    second_head = lax.rem(first_head + 1, H)
    row = lax.broadcasted_iota(jnp.int32, (rows, 128), 0)
    token = row & (K - 1)
    pos_rows = jnp.concatenate([jnp.full((K, 128), pos_ref[s], jnp.int32) for s in range(seqs)], 0)
    acc_rows = jnp.concatenate([jnp.full((K, 128), acc_ref[s], jnp.int32) for s in range(seqs)], 0)
    new_rows = pos_rows + acc_rows
    token_rows = pos_rows + token
    live = token < acc_rows

    def decays(head):
        rate = jnp.sum(jnp.where(head_lane == head, rates, 0.0), axis=1, keepdims=True)
        rate = jnp.broadcast_to(rate, (rows, 128))
        running = rate
        for by in (1, 2, 4):
            running = running + jnp.where(token >= by, pltpu.roll(running, by, 0), 0.0)
        cum = -running
        taken = -jnp.sum(jnp.where(live, rate, 0.0).reshape(seqs, K, 128), axis=1)
        taken_rows = jnp.broadcast_to(taken[:, None, :], (seqs, K, 128)).reshape(rows, 128)
        decay = jnp.where(live, jnp.exp(jnp.minimum(taken_rows - cum, 0.0)), 0.0)
        return cum, jnp.exp(cum), jnp.exp(taken), decay

    cum_a, grown_a, kept_a, decay_a = decays(first_head)
    cum_b, grown_b, kept_b, decay_b = decays(second_head)

    for j in range(LOCAL):
        in_a = j < split
        kept = jnp.where(in_a, kept_a, kept_b)
        occupied = (pos_s >> levels[j]) & 1
        new_occupied = (new_s >> levels[j]) & 1
        above = changed >> levels[j]
        stay_c[j] = jnp.where((above == 0) & (occupied == 1) & (new_occupied == 1), kept, 0.0)
        into_c[j] = jnp.where((above == 1) & (new_occupied == 1), kept, 0.0)

    weights = weights_ref[...].reshape(rows, LOCAL)
    local_lane = lax.broadcasted_iota(jnp.int32, (rows, LOCAL), 1)
    level_lane = lax.rem(level_0 + local_lane, L)
    weight_zero = jnp.sum(jnp.where(level_lane == 0, weights, 0.0), axis=1, keepdims=True)
    quads = (LOCAL + 1) // 2

    def of_lane(q):
        two = 2 * q + jnp.where(lower, 0, 1)
        return jnp.where(lower, levels[2 * q], levels[2 * q + 1]), two < split, two < LOCAL

    padded[:, 0:LOCAL] = weights
    here = lane < LOCAL
    level = level_0 + jnp.where(here, lane, 0)
    level = jnp.where(level >= L, level - L, level)
    shown = here & (((pos_rows >> level) & 1) == 1)
    by_token = jnp.where(shown, padded[...] * jnp.where(lane < split, grown_a, grown_b), 0.0)
    by_level = jnp.transpose(jnp.concatenate([by_token, jnp.zeros_like(by_token)], axis=0))
    by_level = by_level[: LOCAL + 1]
    for s in range(seqs):
        wide_w[s] = jnp.where((lane[: LOCAL + 1] >> 3) == s, by_level, 0.0)
    parts[...] = jnp.zeros_like(parts)

    @pl.when(is_root)
    def _():
        for step in range(1, groups):
            other = lax.rem(sq + step, groups)
            remote(
                counts.at[other], counts.at[other], n_send.at[step], n_recv.at[other], sq, me
            ).wait_recv()
        shared[...] = jnp.sum(counts[...], axis=0)
        for step in range(1, devices):
            total_copy(step).start()

    def await_pieces(indices):
        for index in indices:

            @pl.when(z != first_z + index)
            def _():
                remote(
                    bc.at[index], bc.at[index], y_send.at[0], bc_recv.at[index], sq, me
                ).wait_recv()

        for index in indices:
            if index in others:

                @pl.when(feeds_late)
                def _():
                    late_copy(index).start()

    def vectors(first_feature, indices):
        pair = []
        got = [bc[i].astype(F32) for i in indices]
        for r in range(2):
            part = jnp.zeros((half_rows, 128), F32)
            for i, moved in zip(indices, got):
                start = OWN_IN * (BC_FIRST + i) - first_feature
                by = (start - P_SIZE * r) % 128
                if by:
                    moved = pltpu.roll(moved, by, 1)
                part = jnp.where((half_lane >= start) & (half_lane < start + OWN_IN), moved, part)
            pair.append(part)
        return jnp.concatenate(pair, axis=0)

    await_pieces((2, 3, 4))
    out_vecs = vectors(H * P_SIZE + N, (2, 3, 4))
    across = jnp.transpose(jnp.concatenate([out_vecs, jnp.zeros_like(out_vecs)], axis=0))
    across = across.astype(BF16)
    cc[0:N, :] = across
    cc[N : 2 * N, :] = across

    def read_out(s, carry):
        read = jnp.dot(halves[s], cc[...], preferred_element_type=F32)
        for part in range(3):
            total = parts[part]
            for k in range(block):
                j = part * block + k
                total = total + read[j * P_SIZE : (j + 1) * P_SIZE, :] * wide_w[s, j : j + 1, :]
            parts[part] = total
        return carry

    lax.fori_loop(0, seqs, read_out, 0, unroll=4)

    zero = jnp.zeros((P_SIZE, 128), F32)
    in_a = parts[0] + jnp.where(one_in_a, parts[1], zero) + jnp.where(two_in_a, parts[2], zero)
    in_b = jnp.where(one_in_a, zero, parts[1]) + jnp.where(two_in_a, zero, parts[2])
    readout = jnp.transpose(jnp.concatenate([in_a, in_b], axis=0))[:rows]
    await_pieces((0, 1))
    in_vecs = vectors(H * P_SIZE, (0, 1, 2))

    for gap in gaps:
        index = gap - X_LOW
        source = wrapped(me + gap, devices)
        when(
            needs_values(me, source),
            lambda: remote(
                piece, xs.at[index], x_send.at[index], x_recv.at[index], sq, me
            ).wait_recv(),
        )
    value_parts = []
    for r in range(2):
        part = jnp.zeros((half_rows, 128), F32)
        for gap in range(X_LOW, X_HIGH + 1):
            source = wrapped(me + gap, devices)
            start = value_offset(me, source)
            end = start + jnp.minimum(OWN_IN, H * P_SIZE - OWN_IN * source)
            wanted = needs_values(me, source)
            first = jnp.where(wanted, start, 128)
            by = lax.rem(start + 4 * H * P_SIZE - P_SIZE * r, 128)
            moved = pltpu.roll(xs[gap - X_LOW].astype(F32), by, 1)
            part = jnp.where((half_lane >= first) & (half_lane < end), moved, part)
        value_parts.append(part)
    values = jnp.concatenate(value_parts, axis=0)

    b16 = in_vecs.astype(BF16)
    scores = lax.dot_general(
        out_vecs.astype(BF16),
        jnp.concatenate([b16, b16], axis=0),
        (((1,), (1,)), ((), ())),
        preferred_element_type=F32,
    )
    cum_zero = jnp.where(has_zero_in_a, cum_a, cum_b)
    source_row = lane & (rows - 1)
    cum_across = jnp.sum(jnp.where(source_row == row, cum_zero, 0.0), axis=0, keepdims=True)
    before = ((source_row >> 3) == (row >> 3)) & (source_row <= row)
    mixing = jnp.where(before, jnp.exp(jnp.minimum(cum_zero - cum_across, 0.0)), 0.0) * scores
    high, low = split_two(mixing)
    v16 = values.astype(BF16)
    mixed = jnp.dot(
        jnp.where(lower, high, low).astype(BF16),
        jnp.concatenate([v16, v16], axis=0),
        preferred_element_type=F32,
    )
    zero_here = jnp.where(lower, 1, 0) == as_int(has_zero_in_a)
    drafts = jnp.where(zero_here, mixed * weight_zero, 0.0)

    features = readout + drafts
    held_end = P_SIZE * heads_of(me)

    def packed_for(gap):
        offset = OWN_OUT * wrapped(me + gap, devices) - P_SIZE * first_head
        offset = jnp.where(offset < -(H * P_SIZE) // 2, offset + H * P_SIZE, offset)
        offset = jnp.where(offset > (H * P_SIZE) // 2, offset - H * P_SIZE, offset)
        moved = pltpu.roll(features, lax.rem(4 * H * P_SIZE - offset, 128), 1)
        wanted = (lane < OWN_OUT) & (lane + offset >= 0) & (lane + offset < held_end)
        moved = jnp.where(wanted, moved, 0.0)
        return moved[:half_rows] + pltpu.roll(moved[half_rows:], P_SIZE, 1)

    for index, gap, _, _ in near:
        psend[index] = packed_for(gap)
    for index, gap, sends, _ in near:
        when(sends, lambda: partial_copy(index, gap).start())
    own = packed_for(0)

    turned = pltpu.roll(values, P_SIZE, 1)
    values_a = jnp.where(lower, values, turned) * decay_a
    values_b = jnp.where(lower, turned, values) * decay_b
    b3 = in_vecs.reshape(seqs, K, N)
    bb[...] = jnp.concatenate([b3, b3], axis=1).astype(BF16)
    for q in range(quads):
        level, in_a, real = of_lane(q)
        until = new_rows >> level
        inside = ((until & 1) == 1) & ((token_rows >> level) + 1 == until) & live & real
        term = jnp.where(inside, jnp.where(in_a, values_a, values_b), 0.0)
        high, low = split_two(term)
        both = jnp.concatenate(
            [high.reshape(seqs, K, 128), low.reshape(seqs, K, 128)], axis=1
        )
        xg[:, :, q * 128 : (q + 1) * 128] = both.astype(BF16)

    when(gets_low, lambda: low_copy().wait_recv())

    def update(s, carry):
        tokens = lax.dot_general(
            xg[s], bb[s], (((0,), (0,)), ((), ())), preferred_element_type=F32
        )
        came = jnp.where(gets_low, low_recv[s].astype(F32), 0.0)
        merged_a = low_a[s] + came
        merged_b = low_b[s]
        merged = (
            merged_a,
            jnp.where(split > block, merged_a, merged_b),
            jnp.where(split > 2 * block, merged_a, merged_b),
        )
        for j in range(LOCAL):
            at = slice(j * P_SIZE, (j + 1) * P_SIZE)
            new_ref[s, at, :] = (
                held[s, at, :] * stay_c[j, pl.ds(s, 1), :]
                + merged[j // block] * into_c[j, pl.ds(s, 1), :]
                + tokens[at, :]
            )
        return carry

    lax.fori_loop(0, seqs, update, 0)

    for index, gap, _, gets in near:
        when(
            gets,
            lambda: remote(
                psend.at[index], pslots.at[index], p_send.at[index], p_recv.at[index], sq, me
            ).wait_recv(),
        )
    total = own
    for index, _, _, gets in near:
        came = pslots[index]
        total = total + (came if gets is None else jnp.where(gets, came, 0.0))
    total = jnp.concatenate([total, pltpu.roll(total, P_SIZE, 1)], axis=0)
    out_ref[...] = total.reshape(seqs, K, 128)[:, :, 0:OWN_OUT].astype(BF16)

    @pl.when(me != 0)
    def _():
        remote(shared, shared, t_send.at[0], t_recv.at[0], sq, me).wait_recv()

    share_ref[...] = shared[0:1, 0:1] / (groups * seqs * K)

    @pl.when(is_source)
    def _():
        for r in range(columns - 1):
            y_copy(r).wait_send()

    @pl.when(has_slot)
    def _():
        for step in range(1, ROW):
            when(
                (y != columns - 1) | (lax.rem(z + step, ROW) != LATE),
                lambda: z_copy(step).wait_send(),
            )

    @pl.when(feeds_late)
    def _():
        for index in others:
            late_copy(index).wait_send()

    for gap in gaps:
        when(needs_values(wrapped(me - gap, devices), me), lambda: x_copy(gap).wait_send())
    when(sends_low, lambda: low_copy().wait_send())

    @pl.when(is_root)
    def _():
        for step in range(1, groups):
            count_copy(step).wait_send()
        for step in range(1, devices):
            total_copy(step).wait_send()

    for index, gap, sends, _ in near:
        when(sends, lambda: partial_copy(index, gap).wait_send())


def flush(new_in, out_in, share_in, new_out, out_out, share_out, sems):
    pieces = sems.shape[0] - 2
    size = new_in.shape[0] // pieces
    copies = [
        pltpu.make_async_copy(share_in, share_out, sems.at[pieces]),
        pltpu.make_async_copy(out_in, out_out, sems.at[pieces + 1]),
    ]
    for i in range(pieces):
        at = pl.ds(i * size, size)
        copies.append(pltpu.make_async_copy(new_in.at[at], new_out.at[at], sems.at[i]))
    for copy in copies:
        copy.start()
    for copy in copies:
        copy.wait()


def on_device(states, xbc, rates, level_weights, positions, accepted):
    devices = lax.axis_size("level")
    groups = lax.axis_size("seq")
    seqs = states.shape[0]
    rows = seqs * K
    wide = LOCAL * P_SIZE
    padded_wide = (LOCAL + 1) * P_SIZE
    vmem = pl.BlockSpec(memory_space=pltpu.VMEM)
    in_hbm = pl.BlockSpec(memory_space=pltpu.HBM)
    dma = pltpu.SemaphoreType.DMA
    x_slots = X_HIGH - X_LOW + 1
    outputs, new_states, share = pl.pallas_call(
        functools.partial(kernel, devices, groups),
        out_shape=(
            jax.ShapeDtypeStruct((seqs, K, OWN_OUT), BF16),
            jax.ShapeDtypeStruct((seqs, wide, N), F32),
            jax.ShapeDtypeStruct((1, 1), F32),
        ),
        in_specs=[in_hbm] * 6,
        out_specs=(vmem, vmem, vmem),
        scratch_shapes=[
            pltpu.VMEM(xbc.shape, BF16),
            pltpu.VMEM(rates.shape, F32),
            pltpu.VMEM(level_weights.shape, F32),
            pltpu.SMEM(positions.shape, jnp.int32),
            pltpu.SMEM(accepted.shape, jnp.int32),
            pltpu.VMEM((seqs, wide, N), F32),
            pltpu.VMEM((seqs, wide, 2 * N), BF16),
            pltpu.VMEM((rows, 128), F32),
            pltpu.VMEM((rows // 2, 128), BF16),
            pltpu.VMEM((BC_SLOTS, rows // 2, 128), BF16),
            pltpu.VMEM((x_slots, rows // 2, 128), BF16),
            pltpu.VMEM((seqs, P_SIZE, N), BF16),
            pltpu.VMEM((seqs, P_SIZE, N), BF16),
            pltpu.VMEM((seqs, P_SIZE, N), F32),
            pltpu.VMEM((seqs, P_SIZE, N), F32),
            pltpu.VMEM((LOCAL, seqs, 128), F32),
            pltpu.VMEM((LOCAL, seqs, 128), F32),
            pltpu.VMEM((LOCAL, seqs, 128), F32),
            pltpu.VMEM((seqs, LOCAL + 1, 128), F32),
            pltpu.VMEM((3, P_SIZE, 128), F32),
            pltpu.VMEM((2 * N, 128), BF16),
            pltpu.VMEM((seqs, 2 * K, N), BF16),
            pltpu.VMEM((seqs, 2 * K, padded_wide), BF16),
            pltpu.VMEM((3, rows // 2, 128), F32),
            pltpu.VMEM((3, rows // 2, 128), F32),
            pltpu.VMEM((groups, 8, 128), F32),
            pltpu.VMEM((8, 128), F32),
            dma((5,)),
            dma((seqs,)),
            dma((devices // ROW,)),
            dma((ROW,)),
            dma((x_slots,)),
            dma((BC_SLOTS,)),
            dma((x_slots,)),
            dma((2,)),
            dma((3,)),
            dma((3,)),
            dma((groups,)),
            dma((groups,)),
            dma((BC_SLOTS,)),
            dma((devices,)),
            dma((1,)),
        ],
        compiler_params=pltpu.CompilerParams(
            collective_id=0, has_side_effects=True, vmem_limit_bytes=40 << 20
        ),
    )(
        *[
            pltpu.with_memory_space_constraint(x, pltpu.HBM)
            for x in (
                states.reshape(seqs, wide, N),
                xbc,
                rates,
                level_weights,
                positions,
                accepted,
            )
        ]
    )
    anywhere = pl.BlockSpec(memory_space=pl.ANY)
    new_states, outputs, share = pl.pallas_call(
        flush,
        out_shape=(
            jax.ShapeDtypeStruct(new_states.shape, F32),
            jax.ShapeDtypeStruct(outputs.shape, BF16),
            jax.ShapeDtypeStruct(share.shape, F32),
        ),
        in_specs=[anywhere, anywhere, anywhere],
        out_specs=(in_hbm, in_hbm, in_hbm),
        scratch_shapes=[dma((seqs // 2 + 2,))],
        compiler_params=pltpu.CompilerParams(vmem_limit_bytes=4 << 20),
    )(new_states, outputs, share)
    return outputs, new_states.reshape(states.shape), share.reshape(())


def solution(mesh):
    in_specs = (
        P("seq", "level", None, None),
        P("seq", None, "level"),
        P("seq", None, None),
        P("seq", None, "level"),
        P("seq"),
        P("seq"),
    )
    out_specs = (P("seq", None, "level"), P("seq", "level", None, None), P())
    return jax.shard_map(
        on_device, mesh=mesh, in_specs=in_specs, out_specs=out_specs, check_vma=False
    )
```

```python
import functools

import jax
import jax.numpy as jnp
from jax import lax
from jax.experimental import pallas as pl
from jax.experimental.pallas import tpu as pltpu
from jax.sharding import PartitionSpec as P

H = 24
P_SIZE = 64
N = 128
L = 20
K = 8
ROW = 8
OWN_IN = 56
OWN_OUT = 48
LOCAL = 15
BC_FIRST = 27
BC_SLOTS = 5
LATE = 4
X_LOW, X_HIGH = -5, 2
MESH = pl.DeviceIdType.MESH
F32 = jnp.float32
BF16 = jnp.bfloat16


def first_head_of(d):
    return lax.rem(lax.div(LOCAL * d + L // 2, L), H)


def first_level_of(d):
    return lax.rem(LOCAL * d + L // 2, L)


def heads_of(d):
    return jnp.where(first_level_of(d) + LOCAL > L, 2, 1)


def value_offset(d, s):
    u = OWN_IN * s - P_SIZE * first_head_of(d)
    return jnp.where(u < -(H * P_SIZE) // 2, u + H * P_SIZE, u)


def needs_values(d, s):
    u = value_offset(d, s)
    return (s <= BC_FIRST) & (u > -OWN_IN) & (u < P_SIZE * heads_of(d))


def wrapped(d, devices):
    return lax.rem(d + devices, devices)


def as_int(x):
    return x.astype(jnp.int32)


def split_two(x):
    high = x.astype(BF16).astype(F32)
    return high, x - high


def kernel(
    devices,
    groups,
    states_ref,
    xbc_in,
    rates_in,
    weights_in,
    pos_in,
    acc_in,
    out_ref,
    new_ref,
    share_ref,
    xbc_ref,
    rates_ref,
    weights_ref,
    pos_ref,
    acc_ref,
    held,
    halves,
    padded,
    piece,
    bc,
    xs,
    low_send,
    low_recv,
    low_a,
    low_b,
    leave_c,
    stay_c,
    into_c,
    wide_w,
    parts,
    cc,
    bb,
    xg,
    psend,
    pslots,
    counts,
    shared,
    small_sem,
    in_sem,
    y_send,
    z_send,
    x_send,
    bc_recv,
    x_recv,
    low_sems,
    p_send,
    p_recv,
    n_send,
    n_recv,
    late_send,
    t_send,
    t_recv,
):
    seqs = xbc_ref.shape[0]
    rows = seqs * K
    me = lax.axis_index("level")
    sq = lax.axis_index("seq")
    y, z = lax.div(me, ROW), lax.rem(me, ROW)
    columns = devices // ROW
    first_z = BC_FIRST - (columns - 1) * ROW
    has_slot = z >= first_z
    is_source = has_slot & (y == columns - 1)
    is_late = (y == columns - 1) & (z == LATE)
    feeds_late = (y == 0) & (z == LATE)
    is_root = me == 0
    kind = lax.rem(me, 4)
    slot = jnp.maximum(z - first_z, 0)

    small = [
        pltpu.make_async_copy(src, dst, small_sem.at[i])
        for i, (src, dst) in enumerate(
            (
                (xbc_in, xbc_ref),
                (pos_in, pos_ref),
                (acc_in, acc_ref),
                (rates_in, rates_ref),
                (weights_in, weights_ref),
            )
        )
    ]

    def load(s):
        return pltpu.make_async_copy(states_ref.at[s], held.at[s], in_sem.at[s])

    for copy in small:
        copy.start()
    for s in range(seqs):
        load(s).start()

    barrier = pltpu.get_barrier_semaphore()

    def greet(group, level):
        pl.semaphore_signal(barrier, inc=1, device_id=(group, level), device_id_type=MESH)

    for other in range(first_z, ROW):

        @pl.when((z != other) & ((y != columns - 1) | (z != LATE) | (other == LATE)))
        def _():
            greet(sq, y * ROW + other)

    @pl.when(is_late)
    def _():
        greet(sq, LATE)

    @pl.when(has_slot & (y != columns - 1))
    def _():
        greet(sq, (columns - 1) * ROW + z)

    for gap in range(X_LOW, X_HIGH + 1):
        if gap != 0:
            source = wrapped(me + gap, devices)

            @pl.when(needs_values(me, source))
            def _():
                greet(sq, source)

    greet(sq, wrapped(me - 1, devices))

    @pl.when((kind == 1) | (kind == 2))
    def _():
        greet(sq, wrapped(me - 2, devices))

    @pl.when(kind == 2)
    def _():
        greet(sq, wrapped(me + 1, devices))

    @pl.when(is_root)
    def _():
        for step in range(1, groups):
            greet(lax.rem(sq + step, groups), me)

    @pl.when(me != 0)
    def _():
        greet(sq, 0)

    expected = (ROW - 1) * as_int(has_slot) + (columns - 1) * as_int(is_source) + 1
    expected = expected - as_int(is_source & (z != LATE)) + as_int(feeds_late)
    expected = expected + (devices + groups - 2) * as_int(is_root)
    for gap in range(X_LOW, X_HIGH + 1):
        if gap != 0:
            expected = expected + as_int(needs_values(wrapped(me - gap, devices), me))
    expected = expected + as_int((kind == 0) | (kind == 3)) + as_int(kind == 3)

    lane = lax.broadcasted_iota(jnp.int32, (rows, 128), 1)
    lower = lane < P_SIZE
    half_rows = rows // 2
    half_lane = lane[:half_rows]
    half_lower = half_lane < P_SIZE

    padded[...] = jnp.zeros_like(padded)
    small[0].wait()
    padded[:, 0:OWN_IN] = xbc_ref[...].astype(F32).reshape(rows, OWN_IN)
    wide = padded[...]
    packed = jnp.where(half_lower, wide[:half_rows], pltpu.roll(wide[half_rows:], P_SIZE, 1))
    packed = packed.astype(BF16)
    piece[...] = packed
    xs[-X_LOW] = packed

    @pl.when(is_source)
    def _():
        bc[slot] = packed

    small[1].wait()
    small[2].wait()
    sub = lax.broadcasted_iota(jnp.int32, (seqs, 128), 0)
    pos_s = jnp.zeros((seqs, 128), jnp.int32)
    acc_s = jnp.zeros((seqs, 128), jnp.int32)
    for s in range(seqs):
        pos_s = jnp.where(sub == s, pos_ref[s], pos_s)
        acc_s = jnp.where(sub == s, acc_ref[s], acc_s)
    new_s = pos_s + acc_s
    changed = pos_s ^ new_s
    level_0 = first_level_of(me)
    split = jnp.minimum(L - level_0, LOCAL)
    levels = [lax.rem(level_0 + j, L) for j in range(LOCAL)] + [0]
    block = LOCAL // 3
    one_in_a, two_in_a = split > block, split > 2 * block
    has_zero_in_a = level_0 == 0

    for j in range(LOCAL):
        occupied = (pos_s >> levels[j]) & 1
        above = changed >> levels[j]
        leave_c[j] = jnp.where((above >> 1) != 0, occupied, 0).astype(F32)

    def gather_low(s, carry):
        load(s).wait()
        sums = []
        for part in range(3):
            total = None
            for j in range(part * block, (part + 1) * block):
                x = held[s, j * P_SIZE : (j + 1) * P_SIZE, :]
                high, low = split_two(x)
                halves[s, j * P_SIZE : (j + 1) * P_SIZE, 0:N] = high.astype(BF16)
                halves[s, j * P_SIZE : (j + 1) * P_SIZE, N : 2 * N] = low.astype(BF16)
                term = x * leave_c[j, pl.ds(s, 1), :]
                total = term if total is None else total + term
            sums.append(total)
        zero = jnp.zeros_like(sums[0])
        in_a = sums[0] + jnp.where(one_in_a, sums[1], zero) + jnp.where(two_in_a, sums[2], zero)
        in_b = jnp.where(one_in_a, zero, sums[1]) + jnp.where(two_in_a, zero, sums[2])
        low_a[s] = in_a
        low_b[s] = in_b
        low_send[s] = jnp.where(has_zero_in_a, in_a, in_b).astype(BF16)
        return carry

    @pl.when(jnp.logical_not(is_source))
    def _():
        lax.fori_loop(0, seqs, gather_low, 0)

    @pl.when(is_root)
    def _():
        taken_here = jnp.int32(0)
        for s in range(seqs):
            taken_here = taken_here + acc_ref[s]
        counts[sq] = jnp.full((8, 128), taken_here, jnp.int32).astype(F32)

    pl.semaphore_wait(barrier, expected)

    def remote(src, dst, send_sem, recv_sem, group, level):
        return pltpu.make_async_remote_copy(
            src_ref=src,
            dst_ref=dst,
            send_sem=send_sem,
            recv_sem=recv_sem,
            device_id=(group, level),
            device_id_type=MESH,
        )

    def y_copy(row):
        return remote(bc.at[slot], bc.at[slot], y_send.at[row], bc_recv.at[slot], sq, row * ROW + z)

    def z_copy(step):
        other = y * ROW + lax.rem(z + step, ROW)
        return remote(bc.at[slot], bc.at[slot], z_send.at[step], bc_recv.at[slot], sq, other)

    def x_copy(gap):
        target = wrapped(me - gap, devices)
        index = gap - X_LOW
        return remote(piece, xs.at[index], x_send.at[index], x_recv.at[index], sq, target)

    def low_copy():
        target = wrapped(me + 1, devices)
        return remote(low_send, low_recv, low_sems.at[0], low_sems.at[1], sq, target)

    def count_copy(step):
        return remote(
            counts.at[sq], counts.at[sq], n_send.at[step], n_recv.at[sq], lax.rem(sq + step, groups), me
        )

    others = [index for index in range(BC_SLOTS) if index != LATE - first_z]

    def late_copy(index):
        target = (columns - 1) * ROW + LATE
        return remote(bc.at[index], bc.at[index], late_send.at[index], bc_recv.at[index], sq, target)

    def total_copy(step):
        return remote(shared, shared, t_send.at[step], t_recv.at[0], sq, step)

    def partial_copy(index, gap):
        target = wrapped(me + gap, devices)
        return remote(psend.at[index], pslots.at[index], p_send.at[index], p_recv.at[index], sq, target)

    sends_low = kind != 1
    gets_low = kind != 2
    gaps = [gap for gap in range(X_LOW, X_HIGH + 1) if gap != 0]
    near = (
        (0, 2, (kind == 0) | (kind == 3), (kind == 1) | (kind == 2)),
        (1, 1, None, None),
        (2, -1, kind == 3, kind == 2),
    )

    def when(cond, do):
        if cond is None:
            do()
        else:
            pl.when(cond)(do)

    z_steps = (4, 3, 5, 2, 6, 1, 7)

    @pl.when(is_source)
    def _():
        for r in range(columns - 1):
            y_copy(r).start()
        for step in z_steps:
            when(lax.rem(z + step, ROW) != LATE, lambda: z_copy(step).start())

    for gap in gaps:
        when(needs_values(wrapped(me - gap, devices), me), lambda: x_copy(gap).start())
    @pl.when(is_root)
    def _():
        for step in range(1, groups):
            count_copy(step).start()


    @pl.when(is_source)
    def _():
        lax.fori_loop(0, seqs, gather_low, 0)

    when(sends_low, lambda: low_copy().start())

    @pl.when(has_slot & (y != columns - 1))
    def _():
        remote(bc.at[slot], bc.at[slot], y_send.at[0], bc_recv.at[slot], sq, me).wait_recv()
        for step in z_steps:
            z_copy(step).start()

    head_lane = lax.broadcasted_iota(jnp.int32, (rows, H), 1)
    small[3].wait()
    small[4].wait()
    rates = rates_ref[...].reshape(rows, H)
    first_head = first_head_of(me)
    second_head = lax.rem(first_head + 1, H)
    row = lax.broadcasted_iota(jnp.int32, (rows, 128), 0)
    token = row & (K - 1)
    pos_rows = jnp.concatenate([jnp.full((K, 128), pos_ref[s], jnp.int32) for s in range(seqs)], 0)
    acc_rows = jnp.concatenate([jnp.full((K, 128), acc_ref[s], jnp.int32) for s in range(seqs)], 0)
    new_rows = pos_rows + acc_rows
    token_rows = pos_rows + token
    live = token < acc_rows

    def decays(head):
        rate = jnp.sum(jnp.where(head_lane == head, rates, 0.0), axis=1, keepdims=True)
        rate = jnp.broadcast_to(rate, (rows, 128))
        running = rate
        for by in (1, 2, 4):
            running = running + jnp.where(token >= by, pltpu.roll(running, by, 0), 0.0)
        cum = -running
        taken = -jnp.sum(jnp.where(live, rate, 0.0).reshape(seqs, K, 128), axis=1)
        taken_rows = jnp.broadcast_to(taken[:, None, :], (seqs, K, 128)).reshape(rows, 128)
        decay = jnp.where(live, jnp.exp(jnp.minimum(taken_rows - cum, 0.0)), 0.0)
        return cum, jnp.exp(cum), jnp.exp(taken), decay

    cum_a, grown_a, kept_a, decay_a = decays(first_head)
    cum_b, grown_b, kept_b, decay_b = decays(second_head)

    for j in range(LOCAL):
        in_a = j < split
        kept = jnp.where(in_a, kept_a, kept_b)
        occupied = (pos_s >> levels[j]) & 1
        new_occupied = (new_s >> levels[j]) & 1
        above = changed >> levels[j]
        stay_c[j] = jnp.where((above == 0) & (occupied == 1) & (new_occupied == 1), kept, 0.0)
        into_c[j] = jnp.where((above == 1) & (new_occupied == 1), kept, 0.0)

    weights = weights_ref[...].reshape(rows, LOCAL)
    local_lane = lax.broadcasted_iota(jnp.int32, (rows, LOCAL), 1)
    level_lane = lax.rem(level_0 + local_lane, L)
    weight_zero = jnp.sum(jnp.where(level_lane == 0, weights, 0.0), axis=1, keepdims=True)
    quads = (LOCAL + 1) // 2

    def of_lane(q):
        two = 2 * q + jnp.where(lower, 0, 1)
        return jnp.where(lower, levels[2 * q], levels[2 * q + 1]), two < split, two < LOCAL

    padded[:, 0:LOCAL] = weights
    here = lane < LOCAL
    level = level_0 + jnp.where(here, lane, 0)
    level = jnp.where(level >= L, level - L, level)
    shown = here & (((pos_rows >> level) & 1) == 1)
    by_token = jnp.where(shown, padded[...] * jnp.where(lane < split, grown_a, grown_b), 0.0)
    by_level = jnp.transpose(jnp.concatenate([by_token, jnp.zeros_like(by_token)], axis=0))
    by_level = by_level[: LOCAL + 1]
    for s in range(seqs):
        wide_w[s] = jnp.where((lane[: LOCAL + 1] >> 3) == s, by_level, 0.0)
    parts[...] = jnp.zeros_like(parts)

    @pl.when(is_root)
    def _():
        for step in range(1, groups):
            other = lax.rem(sq + step, groups)
            remote(
                counts.at[other], counts.at[other], n_send.at[step], n_recv.at[other], sq, me
            ).wait_recv()
        shared[...] = jnp.sum(counts[...], axis=0)
        for step in range(1, devices):
            total_copy(step).start()

    def await_pieces(indices):
        for index in indices:

            @pl.when(z != first_z + index)
            def _():
                remote(
                    bc.at[index], bc.at[index], y_send.at[0], bc_recv.at[index], sq, me
                ).wait_recv()

        for index in indices:
            if index in others:

                @pl.when(feeds_late)
                def _():
                    late_copy(index).start()

    def vectors(first_feature, indices):
        pair = []
        got = [bc[i].astype(F32) for i in indices]
        for r in range(2):
            part = jnp.zeros((half_rows, 128), F32)
            for i, moved in zip(indices, got):
                start = OWN_IN * (BC_FIRST + i) - first_feature
                by = (start - P_SIZE * r) % 128
                if by:
                    moved = pltpu.roll(moved, by, 1)
                part = jnp.where((half_lane >= start) & (half_lane < start + OWN_IN), moved, part)
            pair.append(part)
        return jnp.concatenate(pair, axis=0)

    await_pieces((2, 3, 4))
    out_vecs = vectors(H * P_SIZE + N, (2, 3, 4))
    across = jnp.transpose(jnp.concatenate([out_vecs, jnp.zeros_like(out_vecs)], axis=0))
    across = across.astype(BF16)
    cc[0:N, :] = across
    cc[N : 2 * N, :] = across

    def read_out(s, carry):
        read = jnp.dot(halves[s], cc[...], preferred_element_type=F32)
        for part in range(3):
            total = parts[part]
            for k in range(block):
                j = part * block + k
                total = total + read[j * P_SIZE : (j + 1) * P_SIZE, :] * wide_w[s, j : j + 1, :]
            parts[part] = total
        return carry

    lax.fori_loop(0, seqs, read_out, 0, unroll=4)

    zero = jnp.zeros((P_SIZE, 128), F32)
    in_a = parts[0] + jnp.where(one_in_a, parts[1], zero) + jnp.where(two_in_a, parts[2], zero)
    in_b = jnp.where(one_in_a, zero, parts[1]) + jnp.where(two_in_a, zero, parts[2])
    readout = jnp.transpose(jnp.concatenate([in_a, in_b], axis=0))[:rows]
    await_pieces((0, 1))
    in_vecs = vectors(H * P_SIZE, (0, 1, 2))

    for gap in gaps:
        index = gap - X_LOW
        source = wrapped(me + gap, devices)
        when(
            needs_values(me, source),
            lambda: remote(
                piece, xs.at[index], x_send.at[index], x_recv.at[index], sq, me
            ).wait_recv(),
        )
    value_parts = []
    for r in range(2):
        part = jnp.zeros((half_rows, 128), F32)
        for gap in range(X_LOW, X_HIGH + 1):
            source = wrapped(me + gap, devices)
            start = value_offset(me, source)
            end = start + jnp.minimum(OWN_IN, H * P_SIZE - OWN_IN * source)
            wanted = needs_values(me, source)
            first = jnp.where(wanted, start, 128)
            by = lax.rem(start + 4 * H * P_SIZE - P_SIZE * r, 128)
            moved = pltpu.roll(xs[gap - X_LOW].astype(F32), by, 1)
            part = jnp.where((half_lane >= first) & (half_lane < end), moved, part)
        value_parts.append(part)
    values = jnp.concatenate(value_parts, axis=0)

    b16 = in_vecs.astype(BF16)
    scores = lax.dot_general(
        out_vecs.astype(BF16),
        jnp.concatenate([b16, b16], axis=0),
        (((1,), (1,)), ((), ())),
        preferred_element_type=F32,
    )
    cum_zero = jnp.where(has_zero_in_a, cum_a, cum_b)
    source_row = lane & (rows - 1)
    cum_across = jnp.sum(jnp.where(source_row == row, cum_zero, 0.0), axis=0, keepdims=True)
    before = ((source_row >> 3) == (row >> 3)) & (source_row <= row)
    mixing = jnp.where(before, jnp.exp(jnp.minimum(cum_zero - cum_across, 0.0)), 0.0) * scores
    high, low = split_two(mixing)
    v16 = values.astype(BF16)
    mixed = jnp.dot(
        jnp.where(lower, high, low).astype(BF16),
        jnp.concatenate([v16, v16], axis=0),
        preferred_element_type=F32,
    )
    zero_here = jnp.where(lower, 1, 0) == as_int(has_zero_in_a)
    drafts = jnp.where(zero_here, mixed * weight_zero, 0.0)

    features = readout + drafts
    held_end = P_SIZE * heads_of(me)

    def packed_for(gap):
        offset = OWN_OUT * wrapped(me + gap, devices) - P_SIZE * first_head
        offset = jnp.where(offset < -(H * P_SIZE) // 2, offset + H * P_SIZE, offset)
        offset = jnp.where(offset > (H * P_SIZE) // 2, offset - H * P_SIZE, offset)
        moved = pltpu.roll(features, lax.rem(4 * H * P_SIZE - offset, 128), 1)
        wanted = (lane < OWN_OUT) & (lane + offset >= 0) & (lane + offset < held_end)
        moved = jnp.where(wanted, moved, 0.0)
        return moved[:half_rows] + pltpu.roll(moved[half_rows:], P_SIZE, 1)

    for index, gap, _, _ in near:
        psend[index] = packed_for(gap)
    for index, gap, sends, _ in near:
        when(sends, lambda: partial_copy(index, gap).start())
    own = packed_for(0)

    turned = pltpu.roll(values, P_SIZE, 1)
    values_a = jnp.where(lower, values, turned) * decay_a
    values_b = jnp.where(lower, turned, values) * decay_b
    b3 = in_vecs.reshape(seqs, K, N)
    bb[...] = jnp.concatenate([b3, b3], axis=1).astype(BF16)
    for q in range(quads):
        level, in_a, real = of_lane(q)
        until = new_rows >> level
        inside = ((until & 1) == 1) & ((token_rows >> level) + 1 == until) & live & real
        term = jnp.where(inside, jnp.where(in_a, values_a, values_b), 0.0)
        high, low = split_two(term)
        both = jnp.concatenate(
            [high.reshape(seqs, K, 128), low.reshape(seqs, K, 128)], axis=1
        )
        xg[:, :, q * 128 : (q + 1) * 128] = both.astype(BF16)

    when(gets_low, lambda: low_copy().wait_recv())

    def update(s, carry):
        tokens = lax.dot_general(
            xg[s], bb[s], (((0,), (0,)), ((), ())), preferred_element_type=F32
        )
        came = jnp.where(gets_low, low_recv[s].astype(F32), 0.0)
        merged_a = low_a[s] + came
        merged_b = low_b[s]
        merged = (
            merged_a,
            jnp.where(split > block, merged_a, merged_b),
            jnp.where(split > 2 * block, merged_a, merged_b),
        )
        for j in range(LOCAL):
            at = slice(j * P_SIZE, (j + 1) * P_SIZE)
            new_ref[s, at, :] = (
                held[s, at, :] * stay_c[j, pl.ds(s, 1), :]
                + merged[j // block] * into_c[j, pl.ds(s, 1), :]
                + tokens[at, :]
            )
        return carry

    lax.fori_loop(0, seqs, update, 0)

    for index, gap, _, gets in near:
        when(
            gets,
            lambda: remote(
                psend.at[index], pslots.at[index], p_send.at[index], p_recv.at[index], sq, me
            ).wait_recv(),
        )
    total = own
    for index, _, _, gets in near:
        came = pslots[index]
        total = total + (came if gets is None else jnp.where(gets, came, 0.0))
    total = jnp.concatenate([total, pltpu.roll(total, P_SIZE, 1)], axis=0)
    out_ref[...] = total.reshape(seqs, K, 128)[:, :, 0:OWN_OUT].astype(BF16)

    @pl.when(me != 0)
    def _():
        remote(shared, shared, t_send.at[0], t_recv.at[0], sq, me).wait_recv()

    share_ref[...] = shared[0:1, 0:1] / (groups * seqs * K)

    @pl.when(is_source)
    def _():
        for r in range(columns - 1):
            y_copy(r).wait_send()

    @pl.when(has_slot)
    def _():
        for step in range(1, ROW):
            when(
                (y != columns - 1) | (lax.rem(z + step, ROW) != LATE),
                lambda: z_copy(step).wait_send(),
            )

    @pl.when(feeds_late)
    def _():
        for index in others:
            late_copy(index).wait_send()

    for gap in gaps:
        when(needs_values(wrapped(me - gap, devices), me), lambda: x_copy(gap).wait_send())
    when(sends_low, lambda: low_copy().wait_send())

    @pl.when(is_root)
    def _():
        for step in range(1, groups):
            count_copy(step).wait_send()
        for step in range(1, devices):
            total_copy(step).wait_send()

    for index, gap, sends, _ in near:
        when(sends, lambda: partial_copy(index, gap).wait_send())


def flush(new_in, out_in, share_in, new_out, out_out, share_out, sems):
    pieces = sems.shape[0] - 2
    size = new_in.shape[0] // pieces
    copies = [
        pltpu.make_async_copy(share_in, share_out, sems.at[pieces]),
        pltpu.make_async_copy(out_in, out_out, sems.at[pieces + 1]),
    ]
    for i in range(pieces):
        at = pl.ds(i * size, size)
        copies.append(pltpu.make_async_copy(new_in.at[at], new_out.at[at], sems.at[i]))
    for copy in copies:
        copy.start()
    for copy in copies:
        copy.wait()


def on_device(states, xbc, rates, level_weights, positions, accepted):
    devices = lax.axis_size("level")
    groups = lax.axis_size("seq")
    seqs = states.shape[0]
    rows = seqs * K
    wide = LOCAL * P_SIZE
    padded_wide = (LOCAL + 1) * P_SIZE
    vmem = pl.BlockSpec(memory_space=pltpu.VMEM)
    in_hbm = pl.BlockSpec(memory_space=pltpu.HBM)
    dma = pltpu.SemaphoreType.DMA
    x_slots = X_HIGH - X_LOW + 1
    outputs, new_states, share = pl.pallas_call(
        functools.partial(kernel, devices, groups),
        out_shape=(
            jax.ShapeDtypeStruct((seqs, K, OWN_OUT), BF16),
            jax.ShapeDtypeStruct((seqs, wide, N), F32),
            jax.ShapeDtypeStruct((1, 1), F32),
        ),
        in_specs=[in_hbm] * 6,
        out_specs=(vmem, vmem, vmem),
        scratch_shapes=[
            pltpu.VMEM(xbc.shape, BF16),
            pltpu.VMEM(rates.shape, F32),
            pltpu.VMEM(level_weights.shape, F32),
            pltpu.SMEM(positions.shape, jnp.int32),
            pltpu.SMEM(accepted.shape, jnp.int32),
            pltpu.VMEM((seqs, wide, N), F32),
            pltpu.VMEM((seqs, wide, 2 * N), BF16),
            pltpu.VMEM((rows, 128), F32),
            pltpu.VMEM((rows // 2, 128), BF16),
            pltpu.VMEM((BC_SLOTS, rows // 2, 128), BF16),
            pltpu.VMEM((x_slots, rows // 2, 128), BF16),
            pltpu.VMEM((seqs, P_SIZE, N), BF16),
            pltpu.VMEM((seqs, P_SIZE, N), BF16),
            pltpu.VMEM((seqs, P_SIZE, N), F32),
            pltpu.VMEM((seqs, P_SIZE, N), F32),
            pltpu.VMEM((LOCAL, seqs, 128), F32),
            pltpu.VMEM((LOCAL, seqs, 128), F32),
            pltpu.VMEM((LOCAL, seqs, 128), F32),
            pltpu.VMEM((seqs, LOCAL + 1, 128), F32),
            pltpu.VMEM((3, P_SIZE, 128), F32),
            pltpu.VMEM((2 * N, 128), BF16),
            pltpu.VMEM((seqs, 2 * K, N), BF16),
            pltpu.VMEM((seqs, 2 * K, padded_wide), BF16),
            pltpu.VMEM((3, rows // 2, 128), F32),
            pltpu.VMEM((3, rows // 2, 128), F32),
            pltpu.VMEM((groups, 8, 128), F32),
            pltpu.VMEM((8, 128), F32),
            dma((5,)),
            dma((seqs,)),
            dma((devices // ROW,)),
            dma((ROW,)),
            dma((x_slots,)),
            dma((BC_SLOTS,)),
            dma((x_slots,)),
            dma((2,)),
            dma((3,)),
            dma((3,)),
            dma((groups,)),
            dma((groups,)),
            dma((BC_SLOTS,)),
            dma((devices,)),
            dma((1,)),
        ],
        compiler_params=pltpu.CompilerParams(
            collective_id=0, has_side_effects=True, vmem_limit_bytes=40 << 20
        ),
    )(
        *[
            pltpu.with_memory_space_constraint(x, pltpu.HBM)
            for x in (
                states.reshape(seqs, wide, N),
                xbc,
                rates,
                level_weights,
                positions,
                accepted,
            )
        ]
    )
    anywhere = pl.BlockSpec(memory_space=pl.ANY)
    new_states, outputs, share = pl.pallas_call(
        flush,
        out_shape=(
            jax.ShapeDtypeStruct(new_states.shape, F32),
            jax.ShapeDtypeStruct(outputs.shape, BF16),
            jax.ShapeDtypeStruct(share.shape, F32),
        ),
        in_specs=[anywhere, anywhere, anywhere],
        out_specs=(in_hbm, in_hbm, in_hbm),
        scratch_shapes=[dma((seqs + 2,))],
        compiler_params=pltpu.CompilerParams(vmem_limit_bytes=4 << 20),
    )(new_states, outputs, share)
    return outputs, new_states.reshape(states.shape), share.reshape(())


def solution(mesh):
    in_specs = (
        P("seq", "level", None, None),
        P("seq", None, "level"),
        P("seq", None, None),
        P("seq", None, "level"),
        P("seq"),
        P("seq"),
    )
    out_specs = (P("seq", None, "level"), P("seq", "level", None, None), P())
    return jax.shard_map(
        on_device, mesh=mesh, in_specs=in_specs, out_specs=out_specs, check_vma=False
    )
```
